512 devices in a mesh: dp: 2 (over y_lo), tensor: 4 (over x), context: 64 (over z, y_hi, core).
Axes of the slice: x: 4, y: 4 (y_hi: 2, y_lo: 2; y = y_hi * 2 + y_lo), z: 16, core: 2. Of those that a mesh axis runs over, the one named last changes fastest.
Arguments:
- q_in: bfloat16 [2, 8192, 4096], P('dp', 'context', 'tensor'), may hold values from -44 to 44
- k_in: bfloat16 [2, 8192, 4096], P('dp', 'context', 'tensor'), may hold values from -6 to 6
- v_in: bfloat16 [2, 8192, 4096], P('dp', 'context', 'tensor'), may hold values from -6 to 6
- short_filt: float32 [3, 7, 4096], P(None, None, 'tensor'), may hold values from -2 to 2
- long_filt: float32 [8192, 4096], P('context', 'tensor'), may hold values from -1.1 to 1.1
- norm_gain: float32 [4096], P('tensor'), may hold values from 0.1 to 1.9
- grad_out: bfloat16 [2, 8192, 4096], P('dp', 'context', 'tensor'), may hold values from -6 to 6
Outputs:
- mixed: bfloat16 [2, 8192, 4096], P('dp', 'context', 'tensor')
- grad_inputs: bfloat16 [3, 2, 8192, 4096], P(None, 'dp', 'context', 'tensor')
- grad_long: float32 [8192, 4096], P('context', 'tensor')
- grad_short: float32 [3, 7, 4096], P(None, None, 'tensor')
The draws below stay inside these ranges and needn't reach their ends.
All inputs are finite; a program needn't handle non-finite values.
Results may differ from the reference program's by a relative error of at most 0.00225.
Values may be sent and summed in bfloat16 or wider, within the bound.
No kernel may reach another device: no remote copies, remote signals or barrier semaphores. Data moves between devices by JAX's collectives and lax.ppermute only.
A program may use at most 128 MiB of HBM per device.

```python
import math
import jax
import jax.numpy as jnp
from jax import lax

D = 4096
FILT = 7
REPL = 2
SEQ = 8192


def draw_q_in(key, part):
    first, second, third = jax.random.split(jax.random.fold_in(key, 11), 3)
    column = jnp.exp(jax.random.uniform(first, (D,)) * math.log(10.0) * 0.6 + math.log(3.0) * jnp.arange(D, dtype=jnp.float32) / D) / (2.0 * math.sqrt(3.0))
    row_scale = jnp.exp(jax.random.uniform(second, (REPL, SEQ, 1)) * math.log(10.0)) / math.sqrt(10.0)
    noise = jax.random.truncated_normal(third, -4.0, 4.0, (REPL, SEQ, D))
    return (noise * row_scale * column).astype(jnp.bfloat16)


def draw_long_filt(key, part):
    first, second = jax.random.split(jax.random.fold_in(key, 23), 2)
    decay = jnp.exp(jax.random.uniform(first, (D,), minval=math.log(30.0), maxval=math.log(4.0 * SEQ)))
    noise = jax.random.truncated_normal(second, -4.0, 4.0, (SEQ, D))
    position = jnp.arange(SEQ, dtype=jnp.float32)[:, None]
    amplitude = jnp.sqrt(1.0 - jnp.exp(-2.0 / decay))
    return (noise * amplitude * jnp.exp(-position / decay)).astype(jnp.float32)


def steps_of(own_key, extent, pieces, low, high):
    gain = 1.0
    for dim, parts in pieces:
        draws = jax.random.uniform(jax.random.fold_in(jax.random.fold_in(own_key, 6), dim), (parts,), jnp.float32, low / len(pieces), high / len(pieces))
        gain = gain * jnp.repeat(jnp.exp(draws), extent[dim] // parts).reshape((-1,) + (1,) * (len(extent) - 1 - dim))
    return gain


def gaussian(rng, dims, scale, reach, cuts=(), held_as=jnp.bfloat16):
    result = jax.random.normal(rng, dims, jnp.float32) * scale
    if len(cuts) > 0:
        result = steps_of(rng, dims, cuts, -0.22, 0.18) * result
    return jnp.clip(result, min=-reach, max=reach).astype(held_as)


def setup_inputs(seed: int = 0) -> dict:
    key_list = jax.random.split(jax.random.key(seed), 8)
    return {
        "q_in": draw_q_in(jax.random.fold_in(key_list[7], 71), 0),
        "k_in": gaussian(key_list[1], (REPL, SEQ, D), 1.0, 6.0, ((0, 2), (1, 64), (2, 4))),
        "v_in": gaussian(key_list[2], (REPL, SEQ, D), 1.0, 6.0, ((0, 2), (1, 64), (2, 4))),
        "short_filt": gaussian(key_list[3], (3, FILT, D), FILT ** -0.5, 2.0, ((2, 4),), jnp.float32),
        "long_filt": draw_long_filt(jax.random.fold_in(key_list[7], 71), 0),
        "norm_gain": jnp.clip(1.0 + 0.18 * jax.random.normal(key_list[5], (D,), jnp.float32), 0.1, 1.9),
        "grad_out": gaussian(key_list[6], (REPL, SEQ, D), 1.0, 6.0, ((0, 2), (1, 64), (2, 4))),
    }


EPS = 1e-06

def causal_short(seq, filt):
    padded = jnp.pad(seq, ((0, 0), (FILT - 1, 0), (0, 0)))
    total = jnp.zeros(seq.shape, jnp.float32)
    for lag in range(FILT):
        total = total + filt[lag] * padded[:, FILT - 1 - lag:FILT - 1 - lag + SEQ]
    return (total, padded)

def back_short(grads, filt):
    padded = jnp.pad(grads, ((0, 0), (0, FILT - 1), (0, 0)))
    total = jnp.zeros(grads.shape, jnp.float32)
    for lag in range(FILT):
        total = total + filt[lag] * padded[:, lag:lag + SEQ]
    return total

def filter_grads(grads, padded):
    return jnp.stack([lax.optimization_barrier(jnp.sum(grads * padded[:, FILT - 1 - lag:FILT - 1 - lag + SEQ], axis=(0, 1))) for lag in range(FILT)])

def to_blocks(values, width):
    return values.reshape(values.shape[0], SEQ, D // width, width).transpose(2, 0, 1, 3)

def from_blocks(values):
    return values.transpose(1, 2, 0, 3).reshape(values.shape[1], SEQ, D)

def conv_pair(pair):
    kv_block, filt_block = pair
    length = 2 * SEQ
    spec = jnp.fft.rfft(kv_block, n=length, axis=1) * jnp.fft.rfft(filt_block, n=length, axis=0)[None]
    return jnp.fft.irfft(spec, n=length, axis=1)[:, :SEQ]

def back_triple(triple):
    grad_block, kv_block, filt_block = triple
    length = 2 * SEQ
    grad_spec = jnp.fft.rfft(grad_block, n=length, axis=1)
    kv_spec = jnp.fft.rfft(kv_block, n=length, axis=1)
    filt_spec = jnp.fft.rfft(filt_block, n=length, axis=0)[None]
    dkv = jnp.fft.irfft(jnp.conj(filt_spec) * grad_spec, n=length, axis=1)[:, :SEQ]
    dfilt = lax.optimization_barrier(jnp.sum(jnp.fft.irfft(jnp.conj(kv_spec) * grad_spec, n=length, axis=1)[:, :SEQ], axis=0))
    return (dkv, dfilt)

def reference(q_in, k_in, v_in, short_filt, long_filt, norm_gain, grad_out):
    width = math.gcd(D, 256)
    q_short, q_pad = causal_short(q_in.astype(jnp.float32), short_filt[0])
    k_short, k_pad = causal_short(k_in.astype(jnp.float32), short_filt[1])
    v_short, v_pad = causal_short(v_in.astype(jnp.float32), short_filt[2])
    kv = k_short * v_short
    filt_blocks = long_filt.reshape(SEQ, D // width, width).transpose(1, 0, 2)
    conv = from_blocks(lax.map(conv_pair, (to_blocks(kv, width), filt_blocks)))
    y_out = q_short * conv
    rms = jnp.sqrt(lax.optimization_barrier(jnp.mean(y_out * y_out, axis=-1, keepdims=True)) + EPS)
    mixed = (y_out / rms * norm_gain).astype(jnp.bfloat16)
    grad_z = grad_out.astype(jnp.float32) * norm_gain
    prods = lax.optimization_barrier(jnp.sum(grad_z * y_out, axis=-1, keepdims=True))
    grad_y = grad_z / rms - y_out * prods / (D * rms ** 3)
    dconv = grad_y * q_short
    grad_q = grad_y * conv
    dkv_blocks, dfilt_blocks = lax.map(back_triple, (to_blocks(dconv, width), to_blocks(kv, width), filt_blocks))
    dkv = from_blocks(dkv_blocks)
    dfilt = dfilt_blocks.transpose(1, 0, 2).reshape(SEQ, D)
    grad_k = dkv * v_short
    grad_v = dkv * k_short
    scale = 1.0 / math.sqrt(REPL * SEQ)
    grad_inputs = jnp.stack([back_short(grad_q, short_filt[0]), back_short(grad_k, short_filt[1]), back_short(grad_v, short_filt[2])]).astype(jnp.bfloat16)
    grad_short = jnp.stack([filter_grads(grad_q, q_pad), filter_grads(grad_k, k_pad), filter_grads(grad_v, v_pad)]) * scale
    return (mixed, grad_inputs, dfilt * scale, grad_short)
```

```python
import functools
import math

import jax
import jax.numpy as jnp
import numpy as np
from jax import lax
from jax.experimental import pallas as pl
from jax.experimental.pallas import tpu as pltpu
from jax.sharding import PartitionSpec as P

D = 4096
FILT = 7
EPS = 1e-06
LANES = 128
F32 = jnp.float32
BF16 = jnp.bfloat16
VMEM = pl.BlockSpec(memory_space=pltpu.VMEM)
SMEM = pl.BlockSpec(memory_space=pltpu.SMEM)
PARAMS = pltpu.CompilerParams(vmem_limit_bytes=56 * 2**20)


def halves(table):
    high = table.astype(jnp.bfloat16)
    low = (table - high.astype(np.float64)).astype(jnp.bfloat16)
    return high, low


@functools.cache
def tables(rows):
    size = rows * LANES
    row = np.arange(rows)
    lane = np.arange(LANES)
    angle = 2 * np.pi * np.outer(row + 0.25, row) / rows
    high, low = halves(np.concatenate([np.cos(angle), -np.sin(angle)], 0))
    first = np.concatenate([high, high, low], 1)
    high, low = halves(np.concatenate([np.cos(angle).T, -np.sin(angle).T], 1) / size)
    last = np.concatenate([high, high, low], 1)
    turn = 2 * np.pi * np.outer(row + 0.25, lane) / size
    twiddle = np.stack([np.cos(turn), -np.sin(turn)]).astype(np.float32)
    grid = 2 * np.pi * (np.outer(lane, lane) % LANES) / LANES
    cosine, sine = np.cos(grid), -np.sin(grid)
    high, low = halves(np.block([[cosine, sine], [-sine, cosine]]))
    inner = np.concatenate([high, high, low], 0)
    high, low = halves(np.block([[cosine, -sine], [sine, cosine]]))
    outer = np.concatenate([high, high, low], 0)
    return first, last, twiddle, inner, outer


def split(values):
    high = values.astype(BF16)
    return high, (values - high.astype(F32)).astype(BF16)


def dot(left, right):
    return jnp.dot(left, right, preferred_element_type=F32)


def forward(blocks, first_ref, twiddle_ref, inner_ref):
    rows = blocks[0].shape[0]
    real, imag = twiddle_ref[0], twiddle_ref[1]
    parts = []
    for pair in range(0, len(blocks), 2):
        high, low = split(jnp.concatenate(blocks[pair : pair + 2], 1))
        mixed = dot(first_ref[...], jnp.concatenate([high, low, high], 0))
        for side in range(2):
            lanes = slice(side * LANES, (side + 1) * LANES)
            re, im = mixed[:rows, lanes], mixed[rows:, lanes]
            parts.append(jnp.concatenate([re * real - im * imag, re * imag + im * real], 1))
    high, low = split(jnp.concatenate(parts, 0))
    return dot(jnp.concatenate([high, low, high], 1), inner_ref[...])


def inverse(spectra, rows, last_ref, twiddle_ref, outer_ref):
    real, imag = twiddle_ref[0], twiddle_ref[1]
    high, low = split(spectra)
    turned = dot(jnp.concatenate([high, low, high], 1), outer_ref[...])
    count = spectra.shape[0] // rows
    blocks = []
    for pair in range(0, count, 2):
        sides = []
        for block in (pair, pair + 1):
            re = turned[block * rows : (block + 1) * rows, :LANES]
            im = turned[block * rows : (block + 1) * rows, LANES:]
            sides.append(jnp.concatenate([re * real + im * imag, im * real - re * imag], 0))
        high, low = split(jnp.concatenate(sides, 1))
        out = dot(last_ref[...], jnp.concatenate([high, low, high], 0))
        blocks += [out[:, :LANES], out[:, LANES:]]
    return blocks


def times(left, right, conjugate):
    re_l, im_l = left[:, :LANES], left[:, LANES:]
    re_r, im_r = right[:, :LANES], right[:, LANES:]
    if conjugate:
        return jnp.concatenate([re_l * re_r + im_l * im_r, re_l * im_r - im_l * re_r], 1)
    return jnp.concatenate([re_l * re_r - im_l * im_r, re_l * im_r + im_l * re_r], 1)


def lagged(block):
    row = lax.broadcasted_iota(jnp.int32, block.shape, 0)
    lane = lax.broadcasted_iota(jnp.int32, block.shape, 1)
    above = jnp.where(row == 0, 0.0, pltpu.roll(block, 1, 0))
    return [block] + [
        pltpu.roll(jnp.where(lane >= LANES - lag, above, block), lag, 1) for lag in range(1, FILT)
    ]


def led(block):
    rows = block.shape[0]
    row = lax.broadcasted_iota(jnp.int32, block.shape, 0)
    lane = lax.broadcasted_iota(jnp.int32, block.shape, 1)
    below = jnp.where(row == rows - 1, 0.0, pltpu.roll(block, rows - 1, 0))
    return [block] + [
        pltpu.roll(jnp.where(lane < lag, below, block), LANES - lag, 1) for lag in range(1, FILT)
    ]


def filtered(shifted, taps_ref, branch, channel):
    total = shifted[0] * taps_ref[branch * FILT, channel]
    for lag in range(1, FILT):
        total = total + shifted[lag] * taps_ref[branch * FILT + lag, channel]
    return total


def strided(ref, channel, count):
    return ref[pl.ds(channel, ref.shape[0] // count, stride=count), :]


def widen(source_ref, start, count, target_ref):
    rows = source_ref.shape[0]
    target_ref[...] = source_ref[:, start : start + count, :].astype(F32).reshape(rows * count, LANES)


def turn_kernel(count, width, *refs):
    for index, ref in enumerate(refs[:count]):
        out_ref = refs[count]
        for start in range(0, ref.shape[1], LANES):
            block = ref[:, start : start + LANES].astype(F32).T.astype(out_ref.dtype)
            out_ref[start // width : (start + LANES) // width, index * width : (index + 1) * width, :] = (
                block.reshape(LANES // width, width, LANES)
            )


def turn(arrays, width):
    channels = arrays[0].shape[1]
    shape = (channels // width, len(arrays) * width, LANES)
    return pl.pallas_call(
        functools.partial(turn_kernel, len(arrays), width),
        out_shape=jax.ShapeDtypeStruct(shape, arrays[0].dtype),
        in_specs=[VMEM] * len(arrays),
        out_specs=VMEM,
        compiler_params=PARAMS,
    )(*arrays)


def unturn_kernel(count, width, scale, in_ref, *out_refs):
    for index in range(count):
        out_ref = out_refs[index]
        for start in range(0, out_ref.shape[1], LANES):
            block = in_ref[start // width : (start + LANES) // width, index * width : (index + 1) * width, :]
            block = block.astype(F32).reshape(LANES, LANES).T
            if scale is not None:
                block = block * scale
            out_ref[:, start : start + LANES] = block.astype(out_ref.dtype)


def unturn(payload, count, scale=None):
    groups, rows, _ = payload.shape
    width = rows // count
    return pl.pallas_call(
        functools.partial(unturn_kernel, count, width, scale),
        out_shape=[jax.ShapeDtypeStruct((LANES, groups * width), payload.dtype)] * count,
        in_specs=[VMEM],
        out_specs=[VMEM] * count,
        compiler_params=PARAMS,
    )(payload)


STEP = 4


def conv_kernel(width, pair_ref, filt_ref, taps_ref, first_ref, last_ref, twiddle_ref, inner_ref, outer_ref,
                conv_ref, spec_kv_ref, spec_filt_ref, k_ref, v_ref):
    rows = pair_ref.shape[0]
    widen(pair_ref, 0, width, k_ref)
    widen(pair_ref, width, width, v_ref)
    for start in range(0, width, STEP):
        products = []
        filters = []
        for channel in range(start, start + STEP):
            k_short = filtered(lagged(strided(k_ref, channel, width)), taps_ref, 1, channel)
            v_short = filtered(lagged(strided(v_ref, channel, width)), taps_ref, 2, channel)
            products.append(k_short * v_short)
            filters.append(strided(filt_ref, channel, width))
        spec_kv = forward(products, first_ref, twiddle_ref, inner_ref)
        spec_filt = forward(filters, first_ref, twiddle_ref, inner_ref)
        part = slice(start * rows, (start + STEP) * rows)
        spec_kv_ref[part, :] = spec_kv
        spec_filt_ref[part, :] = spec_filt
        convs = inverse(times(spec_kv, spec_filt, False), rows, last_ref, twiddle_ref, outer_ref)
        for index, block in enumerate(convs):
            conv_ref[start + index] = block


def stats_kernel(width, pair_ref, conv_ref, taps_ref, gain_ref, q_short_ref, stats_ref, q_ref, g_ref):
    widen(pair_ref, 0, width, q_ref)
    widen(pair_ref, width, width, g_ref)
    squares = jnp.zeros(stats_ref.shape[1:], F32)
    prods = squares
    for channel in range(width):
        q_short = filtered(lagged(strided(q_ref, channel, width)), taps_ref, 0, channel)
        q_short_ref[channel] = q_short
        y_out = q_short * conv_ref[channel]
        squares = squares + y_out * y_out
        prods = prods + strided(g_ref, channel, width) * gain_ref[0, channel] * y_out
    stats_ref[0] = squares
    stats_ref[1] = prods


def norm_kernel(width, pair_ref, conv_ref, q_short_ref, stats_ref, taps_ref, gain_ref, out_ref, dconv_ref, short_ref,
                q_ref, g_ref, mixed_ref, grad_ref):
    rows = pair_ref.shape[0]
    widen(pair_ref, 0, width, q_ref)
    widen(pair_ref, width, width, g_ref)
    rms = jnp.sqrt(stats_ref[0] / D + EPS)
    inverse_rms = 1.0 / rms
    slope = stats_ref[1] / (D * rms * rms * rms)
    for channel in range(width):
        gain = gain_ref[0, channel]
        q_short = q_short_ref[channel]
        conv = conv_ref[channel]
        y_out = q_short * conv
        mixed_ref[pl.ds(channel, rows, stride=width), :] = y_out / rms * gain
        grad_y = strided(g_ref, channel, width) * gain * inverse_rms - y_out * slope
        dconv_ref[channel] = grad_y * q_short
        grad_q = grad_y * conv
        grad_ref[pl.ds(channel, rows, stride=width), :] = filtered(led(grad_q), taps_ref, 0, channel)
        for lag, block in enumerate(lagged(strided(q_ref, channel, width))):
            short_ref[lag * width + channel : lag * width + channel + 1, :] = jnp.sum(
                grad_q * block, axis=0, keepdims=True
            )
    out_ref[:, :width, :] = mixed_ref[...].reshape(rows, width, LANES).astype(BF16)
    out_ref[:, width:, :] = grad_ref[...].reshape(rows, width, LANES).astype(BF16)


def back_kernel(width, dconv_ref, pair_ref, spec_kv_ref, spec_filt_ref, taps_ref, first_ref, last_ref, twiddle_ref,
                inner_ref, outer_ref, out_ref, dfilt_ref, short_ref, k_ref, v_ref, grad_k_ref, grad_v_ref):
    rows = pair_ref.shape[0]
    widen(pair_ref, 0, width, k_ref)
    widen(pair_ref, width, width, v_ref)
    for start in range(0, width, STEP):
        part = slice(start * rows, (start + STEP) * rows)
        spec = forward(
            [dconv_ref[channel] for channel in range(start, start + STEP)], first_ref, twiddle_ref, inner_ref
        )
        dkv = inverse(times(spec_filt_ref[part, :], spec, True), rows, last_ref, twiddle_ref, outer_ref)
        dfilt = inverse(times(spec_kv_ref[part, :], spec, True), rows, last_ref, twiddle_ref, outer_ref)
        for index in range(STEP):
            channel = start + index
            dfilt_ref[pl.ds(channel, rows, stride=width), :] = dfilt[index]
            k_lags = lagged(strided(k_ref, channel, width))
            v_lags = lagged(strided(v_ref, channel, width))
            grad_k = dkv[index] * filtered(v_lags, taps_ref, 2, channel)
            grad_v = dkv[index] * filtered(k_lags, taps_ref, 1, channel)
            grad_k_ref[pl.ds(channel, rows, stride=width), :] = filtered(led(grad_k), taps_ref, 1, channel)
            grad_v_ref[pl.ds(channel, rows, stride=width), :] = filtered(led(grad_v), taps_ref, 2, channel)
            for lag in range(FILT):
                row = lag * width + channel
                short_ref[row : row + 1, :] = jnp.sum(grad_k * k_lags[lag], axis=0, keepdims=True)
                row += FILT * width
                short_ref[row : row + 1, :] = jnp.sum(grad_v * v_lags[lag], axis=0, keepdims=True)
    out_ref[:, :width, :] = grad_k_ref[...].reshape(rows, width, LANES).astype(BF16)
    out_ref[:, width:, :] = grad_v_ref[...].reshape(rows, width, LANES).astype(BF16)


def exchange(payload):
    return lax.all_to_all(payload, "context", split_axis=0, concat_axis=0, tiled=True)


def swap(half):
    return lax.ppermute(half, "dp", [(0, 1), (1, 0)])


def whole(half, side):
    other = swap(half)
    return jnp.where(
        side == 0, jnp.concatenate([half, other], 1), jnp.concatenate([other, half], 1)
    )


def shards(q_in, k_in, v_in, short_filt, long_filt, norm_gain, grad_out):
    rows = lax.axis_size("context")
    channels = q_in.shape[2]
    width = channels // rows
    size = rows * width
    place = lax.axis_index("context")
    side = lax.axis_index("dp")
    first, last, twiddle, inner, outer = (jnp.asarray(t) for t in tables(rows))
    shape = functools.partial(jax.ShapeDtypeStruct, dtype=F32)
    scratch = pltpu.VMEM((size, LANES), F32)

    taps = lax.dynamic_index_in_dim(short_filt.reshape(3 * FILT, rows, width), place, 1, keepdims=False)
    gain = lax.dynamic_index_in_dim(norm_gain.reshape(rows, width), place, 0)

    filt_own = lax.dynamic_index_in_dim(
        turn([long_filt], width).reshape(rows, 2, width // 2, LANES), side, 1, keepdims=False
    )
    filt_half = exchange(filt_own)
    kv_pair = exchange(turn([k_in[0], v_in[0]], width))
    qg_pair = exchange(turn([q_in[0], grad_out[0]], width))
    filt = whole(filt_half, side).reshape(size, LANES)

    conv, spec_kv, spec_filt = pl.pallas_call(
        functools.partial(conv_kernel, width),
        out_shape=[shape((width, rows, LANES)), shape((size, 2 * LANES)), shape((size, 2 * LANES))],
        in_specs=[VMEM, VMEM, SMEM] + [VMEM] * 5,
        out_specs=[VMEM] * 3,
        scratch_shapes=[scratch] * 2,
        compiler_params=PARAMS,
    )(kv_pair, filt, taps, first, last, twiddle, inner, outer)

    q_short, stats = pl.pallas_call(
        functools.partial(stats_kernel, width),
        out_shape=[shape((width, rows, LANES)), shape((2, rows, LANES))],
        in_specs=[VMEM, VMEM, SMEM, SMEM],
        out_specs=[VMEM] * 2,
        scratch_shapes=[scratch] * 2,
        compiler_params=PARAMS,
    )(qg_pair, conv, taps, gain)
    stats = lax.psum(stats, ("tensor", "context"))

    mixed_pair, dconv, short_q = pl.pallas_call(
        functools.partial(norm_kernel, width),
        out_shape=[
            jax.ShapeDtypeStruct((rows, 2 * width, LANES), BF16),
            shape((width, rows, LANES)),
            shape((FILT * width, LANES)),
        ],
        in_specs=[VMEM] * 4 + [SMEM] * 2,
        out_specs=[VMEM] * 3,
        scratch_shapes=[scratch] * 4,
        compiler_params=PARAMS,
    )(qg_pair, conv, q_short, stats, taps, gain)
    mixed_pair = exchange(mixed_pair)

    grad_pair, dfilt, short_kv = pl.pallas_call(
        functools.partial(back_kernel, width),
        out_shape=[
            jax.ShapeDtypeStruct((rows, 2 * width, LANES), BF16),
            shape((size, LANES)),
            shape((2 * FILT * width, LANES)),
        ],
        in_specs=[VMEM] * 4 + [SMEM] + [VMEM] * 5,
        out_specs=[VMEM] * 3,
        scratch_shapes=[scratch] * 4,
        compiler_params=PARAMS,
    )(dconv, kv_pair, spec_kv, spec_filt, taps, first, last, twiddle, inner, outer)
    grad_pair = exchange(grad_pair)

    scale = 1.0 / math.sqrt(lax.axis_size("dp") * rows * LANES)
    parts = dfilt.reshape(rows, 2, width // 2, LANES)
    own = lax.dynamic_index_in_dim(parts, side, 1, keepdims=False)
    other = lax.dynamic_index_in_dim(parts, 1 - side, 1, keepdims=False)
    dfilt = whole(exchange(own + swap(other)), side)
    (grad_long,) = unturn(dfilt, 1, scale)

    short = jnp.sum(jnp.concatenate([short_q, short_kv]), axis=1) * scale
    short = lax.all_gather(short, ("dp", "context")).reshape(2, rows, 3, FILT, width)
    grad_short = jnp.sum(short, axis=0).transpose(1, 2, 0, 3).reshape(3, FILT, channels)

    mixed, grad_q = unturn(mixed_pair, 2)
    grad_k, grad_v = unturn(grad_pair, 2)
    return (mixed[None], jnp.stack([grad_q, grad_k, grad_v])[:, None], grad_long, grad_short)


def solution(mesh):
    in_specs = (
        P("dp", "context", "tensor"),
        P("dp", "context", "tensor"),
        P("dp", "context", "tensor"),
        P(None, None, "tensor"),
        P("context", "tensor"),
        P("tensor"),
        P("dp", "context", "tensor"),
    )
    out_specs = (
        P("dp", "context", "tensor"),
        P(None, "dp", "context", "tensor"),
        P("context", "tensor"),
        P(None, None, "tensor"),
    )
    return jax.shard_map(shards, mesh=mesh, in_specs=in_specs, out_specs=out_specs, check_vma=False)
```

```python
import functools
import math

import jax
import jax.numpy as jnp
import numpy as np
from jax import lax
from jax.experimental import pallas as pl
from jax.experimental.pallas import tpu as pltpu
from jax.sharding import PartitionSpec as P

D = 4096
FILT = 7
EPS = 1e-06
LANES = 128
F32 = jnp.float32
BF16 = jnp.bfloat16
VMEM = pl.BlockSpec(memory_space=pltpu.VMEM)
SMEM = pl.BlockSpec(memory_space=pltpu.SMEM)
PARAMS = pltpu.CompilerParams(vmem_limit_bytes=56 * 2**20)


def halves(table):
    high = table.astype(jnp.bfloat16)
    low = (table - high.astype(np.float64)).astype(jnp.bfloat16)
    return high, low


@functools.cache
def tables(rows):
    size = rows * LANES
    row = np.arange(rows)
    lane = np.arange(LANES)
    angle = 2 * np.pi * np.outer(row + 0.25, row) / rows
    high, low = halves(np.concatenate([np.cos(angle), -np.sin(angle)], 0))
    first = np.concatenate([high, high, low], 1)
    high, low = halves(np.concatenate([np.cos(angle).T, -np.sin(angle).T], 1) / size)
    last = np.concatenate([high, high, low], 1)
    turn = 2 * np.pi * np.outer(row + 0.25, lane) / size
    twiddle = np.stack([np.cos(turn), -np.sin(turn)]).astype(np.float32)
    grid = 2 * np.pi * (np.outer(lane, lane) % LANES) / LANES
    cosine, sine = np.cos(grid), -np.sin(grid)
    high, low = halves(np.block([[cosine, sine], [-sine, cosine]]))
    inner = np.concatenate([high, high, low], 0)
    high, low = halves(np.block([[cosine, -sine], [sine, cosine]]))
    outer = np.concatenate([high, high, low], 0)
    return first, last, twiddle, inner, outer


def split(values):
    high = values.astype(BF16)
    return high, (values - high.astype(F32)).astype(BF16)


def dot(left, right):
    return jnp.dot(left, right, preferred_element_type=F32)


def forward(blocks, first_ref, twiddle_ref, inner_ref):
    rows = blocks[0].shape[0]
    real, imag = twiddle_ref[0], twiddle_ref[1]
    parts = []
    for pair in range(0, len(blocks), 2):
        high, low = split(jnp.concatenate(blocks[pair : pair + 2], 1))
        mixed = dot(first_ref[...], jnp.concatenate([high, low, high], 0))
        for side in range(2):
            lanes = slice(side * LANES, (side + 1) * LANES)
            re, im = mixed[:rows, lanes], mixed[rows:, lanes]
            parts.append(jnp.concatenate([re * real - im * imag, re * imag + im * real], 1))
    high, low = split(jnp.concatenate(parts, 0))
    return dot(jnp.concatenate([high, low, high], 1), inner_ref[...])


def inverse(spectra, rows, last_ref, twiddle_ref, outer_ref):
    real, imag = twiddle_ref[0], twiddle_ref[1]
    high, low = split(spectra)
    turned = dot(jnp.concatenate([high, low, high], 1), outer_ref[...])
    count = spectra.shape[0] // rows
    blocks = []
    for pair in range(0, count, 2):
        sides = []
        for block in (pair, pair + 1):
            re = turned[block * rows : (block + 1) * rows, :LANES]
            im = turned[block * rows : (block + 1) * rows, LANES:]
            sides.append(jnp.concatenate([re * real + im * imag, im * real - re * imag], 0))
        high, low = split(jnp.concatenate(sides, 1))
        out = dot(last_ref[...], jnp.concatenate([high, low, high], 0))
        blocks += [out[:, :LANES], out[:, LANES:]]
    return blocks


def times(left, right, conjugate):
    re_l, im_l = left[:, :LANES], left[:, LANES:]
    re_r, im_r = right[:, :LANES], right[:, LANES:]
    if conjugate:
        return jnp.concatenate([re_l * re_r + im_l * im_r, re_l * im_r - im_l * re_r], 1)
    return jnp.concatenate([re_l * re_r - im_l * im_r, re_l * im_r + im_l * re_r], 1)


def lagged(block):
    row = lax.broadcasted_iota(jnp.int32, block.shape, 0)
    lane = lax.broadcasted_iota(jnp.int32, block.shape, 1)
    above = jnp.where(row == 0, 0.0, pltpu.roll(block, 1, 0))
    return [block] + [
        pltpu.roll(jnp.where(lane >= LANES - lag, above, block), lag, 1) for lag in range(1, FILT)
    ]


def led(block):
    rows = block.shape[0]
    row = lax.broadcasted_iota(jnp.int32, block.shape, 0)
    lane = lax.broadcasted_iota(jnp.int32, block.shape, 1)
    below = jnp.where(row == rows - 1, 0.0, pltpu.roll(block, rows - 1, 0))
    return [block] + [
        pltpu.roll(jnp.where(lane < lag, below, block), LANES - lag, 1) for lag in range(1, FILT)
    ]


def filtered(shifted, taps_ref, branch, channel):
    total = shifted[0] * taps_ref[branch * FILT, channel]
    for lag in range(1, FILT):
        total = total + shifted[lag] * taps_ref[branch * FILT + lag, channel]
    return total


def strided(ref, start, count, step):
    return ref[pl.ds(start, count, stride=step), :]


def kernel_call(kernel, shapes, smem=(), scratch=(), count=0):
    return pl.pallas_call(
        kernel,
        out_shape=shapes,
        in_specs=[SMEM if index in smem else VMEM for index in range(count)],
        out_specs=[VMEM] * len(shapes),
        scratch_shapes=list(scratch),
        compiler_params=PARAMS,
    )


def f32(*dims):
    return jax.ShapeDtypeStruct(dims, F32)


def bf16(*dims):
    return jax.ShapeDtypeStruct(dims, BF16)


def pack_kernel(width, side_ref, k_ref, v_ref, filt_ref, out_ref):
    low_side = side_ref[0, 0] == 1
    for start in range(0, k_ref.shape[1], LANES):
        into = slice(start // width, (start + LANES) // width)
        for index, ref in enumerate((k_ref, v_ref, filt_ref)):
            block = ref[:, start : start + LANES].astype(F32).T
            if ref is filt_ref:
                block = block - jnp.where(low_side, block.astype(BF16).astype(F32), 0.0)
            out_ref[into, index * width : (index + 1) * width, :] = (
                block.astype(BF16).reshape(LANES // width, width, LANES)
            )


def shifted(values, lag):
    return values[lag : lag + LANES]


HALO = 8


def prepare_kernel(q_ref, halo_ref, grad_ref, taps_ref, gain_ref, q_short_ref, grad_z_ref):
    for start in range(0, q_ref.shape[1], LANES):
        lanes = slice(start, start + LANES)
        extended = jnp.concatenate([halo_ref[:, lanes], q_ref[:, lanes]], 0).astype(F32)
        total = jnp.zeros((LANES, LANES), F32)
        for lag in range(FILT):
            total = total + shifted(extended, HALO - lag) * taps_ref[lag : lag + 1, lanes]
        q_short_ref[lanes, :] = total.T
        grad_z_ref[lanes, :] = (grad_ref[:, lanes].astype(F32) * gain_ref[:, lanes]).T


def conv_kernel(width, groups, payload_ref, taps_ref, first_ref, last_ref, twiddle_ref, inner_ref, outer_ref,
                conv_ref, spec_kv_ref, spec_filt_ref, k_ref, v_ref, filt_ref):
    rows = payload_ref.shape[0] // groups
    span = rows * width
    for index, ref in enumerate((k_ref, v_ref)):
        ref[...] = payload_ref[:, index * width : (index + 1) * width, :].astype(F32).reshape(groups * span, LANES)
    parts = payload_ref[:, 2 * width : 3 * width, :].astype(F32)
    filt_ref[...] = (parts[:rows] + parts[rows:]).reshape(span, LANES)
    for start in range(0, width, 2):
        blocks = []
        for channel in (start, start + 1):
            for group in range(groups):
                place = group * span + channel
                k_short = filtered(lagged(strided(k_ref, place, rows, width)), taps_ref, 1, channel)
                v_short = filtered(lagged(strided(v_ref, place, rows, width)), taps_ref, 2, channel)
                blocks.append(k_short * v_short)
        blocks += [strided(filt_ref, channel, rows, width) for channel in (start, start + 1)]
        spec = forward(blocks, first_ref, twiddle_ref, inner_ref)
        pairs = 2 * groups * rows
        spec_kv, spec_filt = spec[:pairs], spec[pairs:]
        spec_kv_ref[start * groups * rows : (start + 2) * groups * rows, :] = spec_kv
        spec_filt_ref[start * rows : (start + 2) * rows, :] = spec_filt
        products = []
        for side in range(2):
            for group in range(groups):
                block = (side * groups + group) * rows
                products.append(
                    times(spec_kv[block : block + rows], spec_filt[side * rows : (side + 1) * rows], False)
                )
        convs = inverse(jnp.concatenate(products, 0), rows, last_ref, twiddle_ref, outer_ref)
        for side in range(2):
            for group in range(groups):
                conv_ref[pl.ds(group * span + start + side, rows, stride=width), :] = convs[side * groups + group]


def stats_kernel(conv_ref, q_short_ref, grad_z_ref, stats_ref):
    squares = jnp.zeros((LANES, LANES), F32)
    prods = squares
    for start in range(0, conv_ref.shape[0], LANES):
        lanes = slice(start, start + LANES)
        y_out = q_short_ref[lanes, :] * conv_ref[lanes, :]
        squares = squares + y_out * y_out
        prods = prods + grad_z_ref[lanes, :] * y_out
    stats_ref[0:1, :] = jnp.sum(squares, 0, keepdims=True)
    stats_ref[1:2, :] = jnp.sum(prods, 0, keepdims=True)


def scales(stats_ref):
    rms = jnp.sqrt(stats_ref[0:1, :] / D + EPS)
    return rms, stats_ref[1:2, :] / (D * rms * rms * rms)


def dconv_kernel(conv_ref, q_short_ref, grad_z_ref, stats_ref, dconv_ref):
    rms, slope = scales(stats_ref)
    inverse_rms = 1.0 / rms
    for start in range(0, conv_ref.shape[0], LANES):
        lanes = slice(start, start + LANES)
        q_short = q_short_ref[lanes, :]
        y_out = q_short * conv_ref[lanes, :]
        dconv_ref[lanes, :] = (grad_z_ref[lanes, :] * inverse_rms - y_out * slope) * q_short


def norm_kernel(conv_ref, q_short_ref, grad_z_ref, stats_ref, q_ref, halo_ref, gain_ref,
                mixed_ref, grad_ref, edge_ref, short_ref):
    rms, slope = scales(stats_ref)
    inverse_rms = 1.0 / rms
    for start in range(0, conv_ref.shape[0], LANES):
        lanes = slice(start, start + LANES)
        conv = conv_ref[lanes, :]
        y_out = q_short_ref[lanes, :] * conv
        mixed_ref[:, lanes] = ((y_out / rms).T * gain_ref[:, lanes]).astype(BF16)
        grad = ((grad_z_ref[lanes, :] * inverse_rms - y_out * slope) * conv).T
        grad_ref[:, lanes] = grad
        edge_ref[:, lanes] = grad[:HALO]
        extended = jnp.concatenate([halo_ref[:, lanes], q_ref[:, lanes]], 0).astype(F32)
        for lag in range(FILT):
            short_ref[lag : lag + 1, lanes] = jnp.sum(grad * shifted(extended, HALO - lag), 0, keepdims=True)


def grad_q_kernel(grad_ref, edge_ref, taps_ref, out_ref):
    for start in range(0, grad_ref.shape[1], LANES):
        lanes = slice(start, start + LANES)
        extended = jnp.concatenate([grad_ref[:, lanes], edge_ref[:, lanes]], 0)
        total = jnp.zeros((LANES, LANES), F32)
        for lag in range(FILT):
            total = total + shifted(extended, lag) * taps_ref[lag : lag + 1, lanes]
        out_ref[:, lanes] = total.astype(BF16)


def back_kernel(width, groups, scale, dconv_ref, payload_ref, spec_kv_ref, spec_filt_ref, taps_ref, first_ref, last_ref,
                twiddle_ref, inner_ref, outer_ref, out_ref, k_ref, v_ref, grad_k_ref, grad_v_ref, dfilt_ref, short_ref):
    rows = payload_ref.shape[0] // groups
    span = rows * width
    for index, ref in enumerate((k_ref, v_ref)):
        ref[...] = payload_ref[:, index * width : (index + 1) * width, :].astype(F32).reshape(groups * span, LANES)
    short_ref[...] = jnp.zeros(short_ref.shape, F32)
    for start in range(0, width, 2):
        blocks = []
        for channel in (start, start + 1):
            for group in range(groups):
                blocks.append(strided(dconv_ref, group * span + channel, rows, width))
        spec = forward(blocks, first_ref, twiddle_ref, inner_ref)
        spec_filt = spec_filt_ref[start * rows : (start + 2) * rows, :]
        spec_kv = spec_kv_ref[start * groups * rows : (start + 2) * groups * rows, :]
        products = []
        filters = []
        for side in range(2):
            total = 0.0
            for group in range(groups):
                block = (side * groups + group) * rows
                part = spec[block : block + rows]
                products.append(times(spec_filt[side * rows : (side + 1) * rows], part, True))
                total = total + times(spec_kv[block : block + rows], part, True)
            filters.append(total)
        results = inverse(jnp.concatenate(products + filters, 0), rows, last_ref, twiddle_ref, outer_ref)
        for side in range(2):
            channel = start + side
            dfilt_ref[pl.ds(channel, rows, stride=width), :] = results[2 * groups + side] * scale
            for group in range(groups):
                place = group * span + channel
                dkv = results[side * groups + group]
                k_lags = lagged(strided(k_ref, place, rows, width))
                v_lags = lagged(strided(v_ref, place, rows, width))
                grad_k = dkv * filtered(v_lags, taps_ref, 2, channel)
                grad_v = dkv * filtered(k_lags, taps_ref, 1, channel)
                grad_k_ref[pl.ds(place, rows, stride=width), :] = filtered(led(grad_k), taps_ref, 1, channel)
                grad_v_ref[pl.ds(place, rows, stride=width), :] = filtered(led(grad_v), taps_ref, 2, channel)
                for branch, (grad, lags) in enumerate(((grad_k, k_lags), (grad_v, v_lags))):
                    for lag in range(FILT):
                        row = (branch * FILT + lag) * width + channel
                        short_ref[row : row + 1, :] += jnp.sum(grad * lags[lag], axis=0, keepdims=True)
    peers = groups * rows
    out_ref[:, :width, :] = grad_k_ref[...].reshape(peers, width, LANES).astype(BF16)
    out_ref[:, width : 2 * width, :] = grad_v_ref[...].reshape(peers, width, LANES).astype(BF16)
    dfilt = dfilt_ref[...].reshape(rows, width, LANES).astype(BF16)
    short = jnp.sum(short_ref[...].T, axis=0, keepdims=True) * scale
    high = short.astype(BF16).astype(F32)
    row = lax.broadcasted_iota(jnp.int32, (width, LANES), 0)
    short = jnp.where(row == 0, high, jnp.where(row == 1, short - high, 0.0)).astype(BF16)
    short = jnp.broadcast_to(short[None], (rows, width, LANES))
    for group in range(groups):
        into = slice(group * rows, (group + 1) * rows)
        out_ref[into, 2 * width : 3 * width, :] = dfilt
        out_ref[into, 3 * width :, :] = short


def unpack_kernel(width, payload_ref, grad_q_ref, grads_ref, long_ref, short_ref):
    grads_ref[0, 0] = grad_q_ref[...]
    for start in range(0, grad_q_ref.shape[1], LANES):
        lanes = slice(start, start + LANES)
        source = slice(start // width, (start + LANES) // width)
        for index in range(3):
            block = payload_ref[source, index * width : (index + 1) * width, :].astype(F32)
            block = block.reshape(LANES, LANES).T
            if index < 2:
                grads_ref[1 + index, 0, :, lanes] = block.astype(BF16)
            else:
                long_ref[:, lanes] = block
    tail = payload_ref[:, 3 * width :, :].astype(F32)
    short_ref[...] = tail[:, 0, :] + tail[:, 1, :]


def encode(values, top):
    root = jnp.sqrt(jnp.sqrt(jnp.abs(values))) * (60000.0 / top**0.25)
    return jnp.where(values < 0, -root, root).astype(jnp.float16)


def decode(code, top):
    root = code.astype(F32) * (top**0.25 / 60000.0)
    square = root * root
    return jnp.where(root < 0, -square * square, square * square)


PEERS = ("dp", "context")


def exchange(payload):
    return lax.all_to_all(payload, PEERS, split_axis=0, concat_axis=0, tiled=True)


def total_over_peers(values):
    for axis in PEERS:
        size = lax.axis_size(axis)
        bit = 1
        while bit < size:
            values = values + lax.ppermute(values, axis, [(i, i ^ bit) for i in range(size)])
            bit *= 2
    return values


def passed_along(values, by):
    size = lax.axis_size("context")
    pairs = [(i, i + by) for i in range(size) if 0 <= i + by < size]
    return lax.ppermute(values, "context", pairs)


def shards(q_in, k_in, v_in, short_filt, long_filt, norm_gain, grad_out):
    rows = lax.axis_size("context")
    groups = lax.axis_size("dp")
    peers = rows * groups
    channels = q_in.shape[2]
    width = channels // peers
    size = peers * width
    place = lax.axis_index(PEERS)
    first, last, twiddle, inner, outer = (jnp.asarray(t) for t in tables(rows))
    scratch = pltpu.VMEM((size, LANES), F32)
    scale = 1.0 / math.sqrt(groups * rows * LANES)
    gain = norm_gain[None]
    taps_q = jnp.pad(short_filt[0], ((0, 1), (0, 0)))
    taps = lax.dynamic_index_in_dim(short_filt.reshape(3 * FILT, peers, width), place, 1, keepdims=False)

    side = lax.axis_index("dp").astype(jnp.int32).reshape(1, 1)
    (payload,) = kernel_call(
        functools.partial(pack_kernel, width), [bf16(peers, 3 * width, LANES)], smem=(0,), count=4
    )(side, k_in[0], v_in[0], long_filt)
    payload = exchange(payload)

    halo = passed_along(q_in[0, LANES - HALO :], 1)
    q_short, grad_z = kernel_call(prepare_kernel, [f32(channels, LANES)] * 2, count=5)(
        q_in[0], halo, grad_out[0], taps_q, gain
    )

    conv, spec_kv, spec_filt = kernel_call(
        functools.partial(conv_kernel, width, groups),
        [f32(size, LANES), f32(size, 2 * LANES), f32(rows * width, 2 * LANES)],
        smem=(1,),
        scratch=[scratch, scratch, pltpu.VMEM((rows * width, LANES), F32)],
        count=7,
    )(payload, taps, first, last, twiddle, inner, outer)

    conv = exchange(encode(conv, 6.4e7).reshape(peers, width, LANES))
    conv = decode(conv, 6.4e7).reshape(size, LANES)
    (stats,) = kernel_call(stats_kernel, [f32(2, LANES)], count=3)(conv, q_short, grad_z)
    stats = lax.psum(stats, "tensor")
    (dconv,) = kernel_call(dconv_kernel, [f32(size, LANES)], count=4)(conv, q_short, grad_z, stats)
    dconv = exchange(encode(dconv, 4.6e8).reshape(peers, width, LANES))

    mixed, grad_0, edge, short_q = kernel_call(
        norm_kernel,
        [bf16(LANES, channels), f32(LANES, channels), f32(HALO, channels), f32(FILT, channels)],
        count=7,
    )(conv, q_short, grad_z, stats, q_in[0], halo, gain)
    edge = passed_along(edge, -1)
    (grad_q,) = kernel_call(grad_q_kernel, [bf16(LANES, channels)], count=3)(grad_0, edge, taps_q)
    short_q = total_over_peers(short_q) * scale

    dconv = decode(dconv, 4.6e8).reshape(size, LANES)
    (back,) = kernel_call(
        functools.partial(back_kernel, width, groups, scale),
        [bf16(peers, 4 * width, LANES)],
        smem=(4,),
        scratch=[scratch] * 4 + [pltpu.VMEM((rows * width, LANES), F32), pltpu.VMEM((LANES, LANES), F32)],
        count=10,
    )(dconv, payload, spec_kv, spec_filt, taps, first, last, twiddle, inner, outer)
    back = exchange(back)
    grads, grad_long, short = kernel_call(
        functools.partial(unpack_kernel, width),
        [bf16(3, 1, LANES, channels), f32(LANES, channels), f32(peers, LANES)],
        count=2,
    )(back, grad_q)
    short = short[:, : 2 * FILT * width].reshape(peers, 2, FILT, width).transpose(1, 2, 0, 3)
    grad_short = jnp.concatenate([short_q[None], short.reshape(2, FILT, channels)])
    return (mixed[None], grads, grad_long, grad_short)


def solution(mesh):
    in_specs = (
        P("dp", "context", "tensor"),
        P("dp", "context", "tensor"),
        P("dp", "context", "tensor"),
        P(None, None, "tensor"),
        P("context", "tensor"),
        P("tensor"),
        P("dp", "context", "tensor"),
    )
    out_specs = (
        P("dp", "context", "tensor"),
        P(None, "dp", "context", "tensor"),
        P("context", "tensor"),
        P(None, None, "tensor"),
    )
    return jax.shard_map(shards, mesh=mesh, in_specs=in_specs, out_specs=out_specs, check_vma=False)
```

```python
import functools
import math

import jax
import jax.numpy as jnp
import numpy as np
from jax import lax
from jax.experimental import pallas as pl
from jax.experimental.pallas import tpu as pltpu
from jax.sharding import PartitionSpec as P

D = 4096
FILT = 7
EPS = 1e-06
LANES = 128
F32 = jnp.float32
BF16 = jnp.bfloat16
VMEM = pl.BlockSpec(memory_space=pltpu.VMEM)
SMEM = pl.BlockSpec(memory_space=pltpu.SMEM)


def halves(table):
    high = table.astype(jnp.bfloat16)
    low = (table - high.astype(np.float64)).astype(jnp.bfloat16)
    return high, low


@functools.cache
def tables(rows):
    size = rows * LANES
    row = np.arange(rows)
    lane = np.arange(LANES)
    angle = 2 * np.pi * np.outer(row + 0.25, row) / rows
    high, low = halves(np.concatenate([np.cos(angle), -np.sin(angle)], 0))
    first = np.concatenate([high, high, low], 1)
    high, low = halves(np.concatenate([np.cos(angle).T, -np.sin(angle).T], 1) / size)
    last = np.concatenate([high, high, low], 1)
    turn = 2 * np.pi * np.outer(row + 0.25, lane) / size
    twiddle = np.stack([np.cos(turn), -np.sin(turn)]).astype(np.float32)
    grid = 2 * np.pi * (np.outer(lane, lane) % LANES) / LANES
    cosine, sine = np.cos(grid), -np.sin(grid)
    high, low = halves(np.block([[cosine, sine], [-sine, cosine]]))
    inner = np.concatenate([high, high, low], 0)
    high, low = halves(np.block([[cosine, -sine], [sine, cosine]]))
    outer = np.concatenate([high, high, low], 0)
    return first, last, twiddle, inner, outer


def split(values):
    high = values.astype(BF16)
    return high, (values - high.astype(F32)).astype(BF16)


def dot(left, right):
    return jnp.dot(left, right, preferred_element_type=F32)


def forward(blocks, first_ref, twiddle_ref, inner_ref):
    rows = blocks[0].shape[0]
    real, imag = twiddle_ref[0], twiddle_ref[1]
    parts = []
    for pair in range(0, len(blocks), 2):
        high, low = split(jnp.concatenate(blocks[pair : pair + 2], 1))
        mixed = dot(first_ref[...], jnp.concatenate([high, low, high], 0))
        for side in range(2):
            lanes = slice(side * LANES, (side + 1) * LANES)
            re, im = mixed[:rows, lanes], mixed[rows:, lanes]
            parts.append(jnp.concatenate([re * real - im * imag, re * imag + im * real], 1))
    high, low = split(jnp.concatenate(parts, 0))
    return dot(jnp.concatenate([high, low, high], 1), inner_ref[...])


def inverse(spectra, rows, last_ref, twiddle_ref, outer_ref):
    real, imag = twiddle_ref[0], twiddle_ref[1]
    high, low = split(spectra)
    turned = dot(jnp.concatenate([high, low, high], 1), outer_ref[...])
    count = spectra.shape[0] // rows
    blocks = []
    for pair in range(0, count, 2):
        sides = []
        for block in (pair, pair + 1):
            re = turned[block * rows : (block + 1) * rows, :LANES]
            im = turned[block * rows : (block + 1) * rows, LANES:]
            sides.append(jnp.concatenate([re * real + im * imag, im * real - re * imag], 0))
        high, low = split(jnp.concatenate(sides, 1))
        out = dot(last_ref[...], jnp.concatenate([high, low, high], 0))
        blocks += [out[:, :LANES], out[:, LANES:]]
    return blocks


def times(left, right, conjugate):
    re_l, im_l = left[:, :LANES], left[:, LANES:]
    re_r, im_r = right[:, :LANES], right[:, LANES:]
    if conjugate:
        return jnp.concatenate([re_l * re_r + im_l * im_r, re_l * im_r - im_l * re_r], 1)
    return jnp.concatenate([re_l * re_r - im_l * im_r, re_l * im_r + im_l * re_r], 1)


def lagged(block):
    row = lax.broadcasted_iota(jnp.int32, block.shape, 0)
    lane = lax.broadcasted_iota(jnp.int32, block.shape, 1)
    above = jnp.where(row == 0, 0.0, pltpu.roll(block, 1, 0))
    return [block] + [
        pltpu.roll(jnp.where(lane >= LANES - lag, above, block), lag, 1) for lag in range(1, FILT)
    ]


def led(block):
    rows = block.shape[0]
    row = lax.broadcasted_iota(jnp.int32, block.shape, 0)
    lane = lax.broadcasted_iota(jnp.int32, block.shape, 1)
    below = jnp.where(row == rows - 1, 0.0, pltpu.roll(block, rows - 1, 0))
    return [block] + [
        pltpu.roll(jnp.where(lane < lag, below, block), LANES - lag, 1) for lag in range(1, FILT)
    ]


def filtered(shifted, taps_ref, branch, channel):
    total = shifted[0] * taps_ref[branch * FILT, channel]
    for lag in range(1, FILT):
        total = total + shifted[lag] * taps_ref[branch * FILT + lag, channel]
    return total


def strided(ref, start, count, step):
    return ref[pl.ds(start, count, stride=step), :]


def kernel_call(kernel, shapes, smem=(), scratch=(), count=0, mib=6):
    return pl.pallas_call(
        kernel,
        out_shape=shapes,
        in_specs=[SMEM if index in smem else VMEM for index in range(count)],
        out_specs=[VMEM] * len(shapes),
        scratch_shapes=list(scratch),
        compiler_params=pltpu.CompilerParams(vmem_limit_bytes=mib * 2**20),
    )


def f32(*dims):
    return jax.ShapeDtypeStruct(dims, F32)


def bf16(*dims):
    return jax.ShapeDtypeStruct(dims, BF16)


def pack_kernel(width, side_ref, k_ref, v_ref, filt_ref, out_ref):
    low_side = side_ref[0, 0] == 1
    for start in range(0, k_ref.shape[1], LANES):
        into = slice(start // width, (start + LANES) // width)
        for index, ref in enumerate((k_ref, v_ref, filt_ref)):
            block = ref[:, start : start + LANES].astype(F32).T
            if ref is filt_ref:
                block = block - jnp.where(low_side, block.astype(BF16).astype(F32), 0.0)
            out_ref[into, index * width : (index + 1) * width, :] = (
                block.astype(BF16).reshape(LANES // width, width, LANES)
            )


def shifted(values, lag):
    return values[lag : lag + LANES]


HALO = 8


def prepare_kernel(q_ref, halo_ref, grad_ref, taps_ref, gain_ref, q_short_ref, grad_z_ref):
    for start in range(0, q_ref.shape[1], LANES):
        lanes = slice(start, start + LANES)
        extended = jnp.concatenate([halo_ref[:, lanes], q_ref[:, lanes]], 0).astype(F32)
        total = jnp.zeros((LANES, LANES), F32)
        for lag in range(FILT):
            total = total + shifted(extended, HALO - lag) * taps_ref[lag : lag + 1, lanes]
        q_short_ref[lanes, :] = total.T
        grad_z_ref[lanes, :] = (grad_ref[:, lanes].astype(F32) * gain_ref[:, lanes]).T


def conv_kernel(width, groups, payload_ref, taps_ref, first_ref, last_ref, twiddle_ref, inner_ref, outer_ref,
                conv_ref, spec_kv_ref, spec_filt_ref, k_ref, v_ref, filt_ref):
    rows = payload_ref.shape[0] // groups
    span = rows * width
    for index, ref in enumerate((k_ref, v_ref)):
        ref[...] = payload_ref[:, index * width : (index + 1) * width, :].astype(F32).reshape(groups * span, LANES)
    parts = payload_ref[:, 2 * width : 3 * width, :].astype(F32)
    filt_ref[...] = (parts[:rows] + parts[rows:]).reshape(span, LANES)
    for start in range(0, width, 2):
        blocks = []
        for channel in (start, start + 1):
            for group in range(groups):
                place = group * span + channel
                k_short = filtered(lagged(strided(k_ref, place, rows, width)), taps_ref, 1, channel)
                v_short = filtered(lagged(strided(v_ref, place, rows, width)), taps_ref, 2, channel)
                blocks.append(k_short * v_short)
        blocks += [strided(filt_ref, channel, rows, width) for channel in (start, start + 1)]
        spec = forward(blocks, first_ref, twiddle_ref, inner_ref)
        pairs = 2 * groups * rows
        spec_kv, spec_filt = spec[:pairs], spec[pairs:]
        spec_kv_ref[start * groups * rows : (start + 2) * groups * rows, :] = spec_kv
        spec_filt_ref[start * rows : (start + 2) * rows, :] = spec_filt
        products = []
        for side in range(2):
            for group in range(groups):
                block = (side * groups + group) * rows
                products.append(
                    times(spec_kv[block : block + rows], spec_filt[side * rows : (side + 1) * rows], False)
                )
        convs = inverse(jnp.concatenate(products, 0), rows, last_ref, twiddle_ref, outer_ref)
        for side in range(2):
            for group in range(groups):
                conv_ref[pl.ds(group * span + start + side, rows, stride=width), :] = convs[side * groups + group]


def stats_kernel(conv_ref, q_short_ref, grad_z_ref, stats_ref):
    squares = jnp.zeros((LANES, LANES), F32)
    prods = squares
    for start in range(0, conv_ref.shape[0], LANES):
        lanes = slice(start, start + LANES)
        y_out = q_short_ref[lanes, :] * conv_ref[lanes, :]
        squares = squares + y_out * y_out
        prods = prods + grad_z_ref[lanes, :] * y_out
    squares = jnp.sum(squares, 0, keepdims=True)
    prods = jnp.sum(prods, 0, keepdims=True)
    for peer in range(stats_ref.shape[0]):
        stats_ref[peer, 0:1, :] = squares
        stats_ref[peer, 1:2, :] = prods


def scales(stats_ref):
    stats = jnp.sum(stats_ref[...], axis=0)
    rms = jnp.sqrt(stats[0:1] / D + EPS)
    return rms, stats[1:2] / (D * rms * rms * rms)


def dconv_kernel(conv_ref, q_short_ref, grad_z_ref, stats_ref, dconv_ref):
    rms, slope = scales(stats_ref)
    inverse_rms = 1.0 / rms
    for start in range(0, conv_ref.shape[0], LANES):
        lanes = slice(start, start + LANES)
        q_short = q_short_ref[lanes, :]
        y_out = q_short * conv_ref[lanes, :]
        dconv_ref[lanes, :] = (grad_z_ref[lanes, :] * inverse_rms - y_out * slope) * q_short


def norm_kernel(conv_ref, q_short_ref, grad_z_ref, stats_ref, q_ref, halo_ref, gain_ref,
                mixed_ref, grad_ref, edge_ref, short_ref):
    rms, slope = scales(stats_ref)
    inverse_rms = 1.0 / rms
    for start in range(0, conv_ref.shape[0], LANES):
        lanes = slice(start, start + LANES)
        conv = conv_ref[lanes, :]
        y_out = q_short_ref[lanes, :] * conv
        mixed_ref[:, lanes] = ((y_out / rms).T * gain_ref[:, lanes]).astype(BF16)
        grad = ((grad_z_ref[lanes, :] * inverse_rms - y_out * slope) * conv).T
        grad_ref[:, lanes] = grad
        edge_ref[:, lanes] = grad[:HALO]
        extended = jnp.concatenate([halo_ref[:, lanes], q_ref[:, lanes]], 0).astype(F32)
        for lag in range(FILT):
            short_ref[lag : lag + 1, lanes] = jnp.sum(grad * shifted(extended, HALO - lag), 0, keepdims=True)


def grad_q_kernel(grad_ref, edge_ref, taps_ref, out_ref):
    for start in range(0, grad_ref.shape[1], LANES):
        lanes = slice(start, start + LANES)
        extended = jnp.concatenate([grad_ref[:, lanes], edge_ref[:, lanes]], 0)
        total = jnp.zeros((LANES, LANES), F32)
        for lag in range(FILT):
            total = total + shifted(extended, lag) * taps_ref[lag : lag + 1, lanes]
        out_ref[:, lanes] = total.astype(BF16)


def back_kernel(width, groups, scale, dconv_ref, payload_ref, spec_kv_ref, spec_filt_ref, taps_ref, first_ref, last_ref,
                twiddle_ref, inner_ref, outer_ref, out_ref, k_ref, v_ref, grad_k_ref, grad_v_ref, dfilt_ref, short_ref):
    rows = payload_ref.shape[0] // groups
    span = rows * width
    part_width = width // groups
    for index, ref in enumerate((k_ref, v_ref)):
        ref[...] = payload_ref[:, index * width : (index + 1) * width, :].astype(F32).reshape(groups * span, LANES)
    short_ref[...] = jnp.zeros(short_ref.shape, F32)
    dfilt_ref[...] = jnp.zeros(dfilt_ref.shape, F32)
    for start in range(0, width, 2):
        blocks = []
        for channel in (start, start + 1):
            for group in range(groups):
                blocks.append(strided(dconv_ref, group * span + channel, rows, width))
        spec = forward(blocks, first_ref, twiddle_ref, inner_ref)
        spec_filt = spec_filt_ref[start * rows : (start + 2) * rows, :]
        spec_kv = spec_kv_ref[start * groups * rows : (start + 2) * groups * rows, :]
        products = []
        filters = []
        for side in range(2):
            total = 0.0
            for group in range(groups):
                block = (side * groups + group) * rows
                part = spec[block : block + rows]
                products.append(times(spec_filt[side * rows : (side + 1) * rows], part, True))
                total = total + times(spec_kv[block : block + rows], part, True)
            filters.append(total)
        results = inverse(jnp.concatenate(products + filters, 0), rows, last_ref, twiddle_ref, outer_ref)
        for side in range(2):
            channel = start + side
            target = channel // part_width * span + channel % part_width
            dfilt_ref[pl.ds(target, rows, stride=width), :] = results[2 * groups + side] * scale
            for group in range(groups):
                place = group * span + channel
                dkv = results[side * groups + group]
                k_lags = lagged(strided(k_ref, place, rows, width))
                v_lags = lagged(strided(v_ref, place, rows, width))
                grad_k = dkv * filtered(v_lags, taps_ref, 2, channel)
                grad_v = dkv * filtered(k_lags, taps_ref, 1, channel)
                grad_k_ref[pl.ds(place, rows, stride=width), :] = filtered(led(grad_k), taps_ref, 1, channel)
                grad_v_ref[pl.ds(place, rows, stride=width), :] = filtered(led(grad_v), taps_ref, 2, channel)
                for branch, (grad, lags) in enumerate(((grad_k, k_lags), (grad_v, v_lags))):
                    for lag in range(FILT):
                        row = (branch * FILT + lag) * width + channel
                        short_ref[row : row + 1, :] += jnp.sum(grad * lags[lag], axis=0, keepdims=True)
    peers = groups * rows
    out_ref[:, :width, :] = grad_k_ref[...].reshape(peers, width, LANES).astype(BF16)
    out_ref[:, width : 2 * width, :] = grad_v_ref[...].reshape(peers, width, LANES).astype(BF16)
    short = jnp.sum(short_ref[...].T, axis=0, keepdims=True) * scale
    high = short.astype(BF16).astype(F32)
    for row, values in enumerate((high, short - high)):
        dfilt_ref[pl.ds(part_width + row, peers, stride=width), :] = jnp.broadcast_to(values, (peers, LANES))
    out_ref[:, 2 * width :, :] = dfilt_ref[...].reshape(peers, width, LANES).astype(BF16)


def part_kernel(width, part_width, payload_ref, part_ref, short_ref, rows_ref, out_ref):
    peers = payload_ref.shape[0]
    rows_ref[...] = payload_ref[:, 2 * width :, :].astype(F32).reshape(peers * width, LANES)
    for row in range(part_width):
        out_ref[pl.ds(row, peers, stride=part_width), :] = strided(rows_ref, row, peers, width)
    part_ref[...] = out_ref[...].astype(BF16)
    short_ref[...] = strided(rows_ref, part_width, peers, width) + strided(rows_ref, part_width + 1, peers, width)


def unpack_kernel(width, payload_ref, grad_q_ref, grads_ref):
    grads_ref[0, 0] = grad_q_ref[...]
    for start in range(0, grad_q_ref.shape[1], LANES):
        source = slice(start // width, (start + LANES) // width)
        for index in range(2):
            block = payload_ref[source, index * width : (index + 1) * width, :].astype(F32)
            grads_ref[1 + index, 0, :, start : start + LANES] = block.reshape(LANES, LANES).T.astype(BF16)


def join_kernel(width, part_width, side_ref, own_ref, other_ref, long_ref, from_ref, rows_ref):
    peers = long_ref.shape[1] // width
    for order, ref in ((side_ref[0, 0], own_ref), (1 - side_ref[0, 0], other_ref)):
        from_ref[...] = ref[...].astype(F32)
        for row in range(part_width):
            rows_ref[pl.ds(order * part_width + row, peers, stride=width), :] = strided(
                from_ref, row, peers, part_width
            )
    for start in range(0, long_ref.shape[1], LANES):
        long_ref[:, start : start + LANES] = rows_ref[start : start + LANES, :].T


def encode(values, top):
    root = jnp.sqrt(jnp.sqrt(jnp.abs(values))) * (60000.0 / top**0.25)
    return jnp.where(values < 0, -root, root).astype(jnp.float16)


def decode(code, top):
    root = code.astype(F32) * (top**0.25 / 60000.0)
    square = root * root
    return jnp.where(root < 0, -square * square, square * square)


PEERS = ("dp", "context")


def exchange(payload):
    return lax.all_to_all(payload, PEERS, split_axis=0, concat_axis=0, tiled=True)


def paired_sum(values, axis, bit):
    return values + lax.ppermute(values, axis, [(i, i ^ bit) for i in range(lax.axis_size(axis))])


def passed_along(values, by):
    size = lax.axis_size("context")
    pairs = [(i, i + by) for i in range(size) if 0 <= i + by < size]
    return lax.ppermute(values, "context", pairs)


def shards(q_in, k_in, v_in, short_filt, long_filt, norm_gain, grad_out):
    rows = lax.axis_size("context")
    groups = lax.axis_size("dp")
    peers = rows * groups
    channels = q_in.shape[2]
    width = channels // peers
    size = peers * width
    place = lax.axis_index(PEERS)
    first, last, twiddle, inner, outer = (jnp.asarray(t) for t in tables(rows))
    scratch = pltpu.VMEM((size, LANES), F32)
    scale = 1.0 / math.sqrt(groups * rows * LANES)
    gain = norm_gain[None]
    taps_q = jnp.pad(short_filt[0], ((0, 1), (0, 0)))
    taps = lax.dynamic_index_in_dim(short_filt.reshape(3 * FILT, peers, width), place, 1, keepdims=False)

    side = lax.axis_index("dp").astype(jnp.int32).reshape(1, 1)
    (payload,) = kernel_call(
        functools.partial(pack_kernel, width), [bf16(peers, 3 * width, LANES)], smem=(0,), count=4
    )(side, k_in[0], v_in[0], long_filt)
    payload = exchange(payload)

    halo = passed_along(q_in[0, LANES - HALO :], 1)
    q_short, grad_z = kernel_call(prepare_kernel, [f32(channels, LANES)] * 2, count=5)(
        q_in[0], halo, grad_out[0], taps_q, gain
    )

    conv, spec_kv, spec_filt = kernel_call(
        functools.partial(conv_kernel, width, groups),
        [f32(size, LANES), f32(size, 2 * LANES), f32(rows * width, 2 * LANES)],
        smem=(1,),
        scratch=[scratch, scratch, pltpu.VMEM((rows * width, LANES), F32)],
        count=7,
        mib=10,
    )(payload, taps, first, last, twiddle, inner, outer)

    conv = exchange(encode(conv, 6.4e7).reshape(peers, width, LANES))
    conv = decode(conv, 6.4e7).reshape(size, LANES)
    (stats,) = kernel_call(stats_kernel, [f32(lax.axis_size("tensor"), 2, LANES)], count=3)(conv, q_short, grad_z)
    stats = lax.all_to_all(stats, "tensor", split_axis=0, concat_axis=0, tiled=True)
    (dconv,) = kernel_call(dconv_kernel, [f32(size, LANES)], count=4)(conv, q_short, grad_z, stats)
    dconv = exchange(encode(dconv, 4.6e8).reshape(peers, width, LANES))

    mixed, grad_0, edge, short_q = kernel_call(
        norm_kernel,
        [bf16(LANES, channels), f32(LANES, channels), f32(HALO, channels), f32(FILT, channels)],
        count=7,
    )(conv, q_short, grad_z, stats, q_in[0], halo, gain)
    edge = passed_along(edge, -1)
    for bit in range(groups.bit_length() - 1):
        short_q = paired_sum(short_q, "dp", 1 << bit)
    short_q = paired_sum(short_q, "context", 1)
    dconv, mixed, grad_0, edge, short_q = lax.optimization_barrier((dconv, mixed, grad_0, edge, short_q))
    (grad_q,) = kernel_call(grad_q_kernel, [bf16(LANES, channels)], count=3)(grad_0, edge, taps_q)
    for bit in range(1, rows.bit_length() - 1):
        short_q = paired_sum(short_q, "context", 1 << bit)

    dconv = decode(dconv, 4.6e8).reshape(size, LANES)
    (back,) = kernel_call(
        functools.partial(back_kernel, width, groups, scale),
        [bf16(peers, 3 * width, LANES)],
        smem=(4,),
        scratch=[scratch] * 5 + [pltpu.VMEM((LANES, LANES), F32)],
        count=10,
        mib=10,
    )(dconv, payload, spec_kv, spec_filt, taps, first, last, twiddle, inner, outer)
    back = exchange(back)
    part_width = width // groups
    part_scratch = pltpu.VMEM((peers * part_width, LANES), F32)
    part, short = kernel_call(
        functools.partial(part_kernel, width, part_width),
        [bf16(peers * part_width, LANES), f32(peers, LANES)],
        scratch=[scratch, part_scratch],
        count=1,
    )(back)
    other = lax.ppermute(part, "dp", [(i, i ^ 1) for i in range(groups)])
    (grads,) = kernel_call(
        functools.partial(unpack_kernel, width), [bf16(3, 1, LANES, channels)], count=2
    )(back, grad_q)
    (grad_long,) = kernel_call(
        functools.partial(join_kernel, width, part_width),
        [f32(LANES, channels)],
        smem=(0,),
        scratch=[part_scratch, scratch],
        count=3,
    )(side, part, other)
    short = short[:, : 2 * FILT * width].reshape(peers, 2, FILT, width).transpose(1, 2, 0, 3)
    grad_short = jnp.concatenate([short_q[None] * scale, short.reshape(2, FILT, channels)])
    return (mixed[None], grads, grad_long, grad_short)


def solution(mesh):
    in_specs = (
        P("dp", "context", "tensor"),
        P("dp", "context", "tensor"),
        P("dp", "context", "tensor"),
        P(None, None, "tensor"),
        P("context", "tensor"),
        P("tensor"),
        P("dp", "context", "tensor"),
    )
    out_specs = (
        P("dp", "context", "tensor"),
        P(None, "dp", "context", "tensor"),
        P("context", "tensor"),
        P(None, None, "tensor"),
    )
    return jax.shard_map(shards, mesh=mesh, in_specs=in_specs, out_specs=out_specs, check_vma=False)
```

```python
import functools
import math

import jax
import jax.numpy as jnp
import numpy as np
from jax import lax
from jax.experimental import pallas as pl
from jax.experimental.pallas import tpu as pltpu
from jax.sharding import PartitionSpec as P

D = 4096
FILT = 7
EPS = 1e-06
LANES = 128
F32 = jnp.float32
BF16 = jnp.bfloat16
VMEM = pl.BlockSpec(memory_space=pltpu.VMEM)
SMEM = pl.BlockSpec(memory_space=pltpu.SMEM)


def halves(table):
    high = table.astype(jnp.bfloat16)
    low = (table - high.astype(np.float64)).astype(jnp.bfloat16)
    return high, low


@functools.cache
def tables(rows):
    size = rows * LANES
    row = np.arange(rows)
    lane = np.arange(LANES)
    angle = 2 * np.pi * np.outer(row + 0.25, row) / rows
    high, low = halves(np.concatenate([np.cos(angle), -np.sin(angle)], 0))
    first = np.concatenate([high, high, low], 1)
    high, low = halves(np.concatenate([np.cos(angle).T, -np.sin(angle).T], 1) / size)
    last = np.concatenate([high, high, low], 1)
    turn = 2 * np.pi * np.outer(row + 0.25, lane) / size
    twiddle = np.stack([np.cos(turn), -np.sin(turn)]).astype(np.float32)
    grid = 2 * np.pi * (np.outer(lane, lane) % LANES) / LANES
    cosine, sine = np.cos(grid), -np.sin(grid)
    high, low = halves(np.block([[cosine, sine], [-sine, cosine]]))
    inner = np.concatenate([high, high, low], 0)
    high, low = halves(np.block([[cosine, -sine], [sine, cosine]]))
    outer = np.concatenate([high, high, low], 0)
    return first, last, twiddle, inner, outer


def split(values):
    high = values.astype(BF16)
    return high, (values - high.astype(F32)).astype(BF16)


def dot(left, right):
    return jnp.dot(left, right, preferred_element_type=F32)


def forward(blocks, first_ref, twiddle_ref, inner_ref):
    rows = blocks[0].shape[0]
    real, imag = twiddle_ref[0], twiddle_ref[1]
    parts = []
    for pair in range(0, len(blocks), 2):
        high, low = split(jnp.concatenate(blocks[pair : pair + 2], 1))
        mixed = dot(first_ref[...], jnp.concatenate([high, low, high], 0))
        for side in range(2):
            lanes = slice(side * LANES, (side + 1) * LANES)
            re, im = mixed[:rows, lanes], mixed[rows:, lanes]
            parts.append(jnp.concatenate([re * real - im * imag, re * imag + im * real], 1))
    high, low = split(jnp.concatenate(parts, 0))
    return dot(jnp.concatenate([high, low, high], 1), inner_ref[...])


def inverse(spectra, rows, last_ref, twiddle_ref, outer_ref):
    real, imag = twiddle_ref[0], twiddle_ref[1]
    high, low = split(spectra)
    turned = dot(jnp.concatenate([high, low, high], 1), outer_ref[...])
    count = spectra.shape[0] // rows
    blocks = []
    for pair in range(0, count, 2):
        sides = []
        for block in (pair, pair + 1):
            re = turned[block * rows : (block + 1) * rows, :LANES]
            im = turned[block * rows : (block + 1) * rows, LANES:]
            sides.append(jnp.concatenate([re * real + im * imag, im * real - re * imag], 0))
        high, low = split(jnp.concatenate(sides, 1))
        out = dot(last_ref[...], jnp.concatenate([high, low, high], 0))
        blocks += [out[:, :LANES], out[:, LANES:]]
    return blocks


def times(left, right, conjugate):
    re_l, im_l = left[:, :LANES], left[:, LANES:]
    re_r, im_r = right[:, :LANES], right[:, LANES:]
    if conjugate:
        return jnp.concatenate([re_l * re_r + im_l * im_r, re_l * im_r - im_l * re_r], 1)
    return jnp.concatenate([re_l * re_r - im_l * im_r, re_l * im_r + im_l * re_r], 1)


def lagged(block):
    row = lax.broadcasted_iota(jnp.int32, block.shape, 0)
    lane = lax.broadcasted_iota(jnp.int32, block.shape, 1)
    above = jnp.where(row == 0, 0.0, pltpu.roll(block, 1, 0))
    return [block] + [
        pltpu.roll(jnp.where(lane >= LANES - lag, above, block), lag, 1) for lag in range(1, FILT)
    ]


def led(block):
    rows = block.shape[0]
    row = lax.broadcasted_iota(jnp.int32, block.shape, 0)
    lane = lax.broadcasted_iota(jnp.int32, block.shape, 1)
    below = jnp.where(row == rows - 1, 0.0, pltpu.roll(block, rows - 1, 0))
    return [block] + [
        pltpu.roll(jnp.where(lane < lag, below, block), LANES - lag, 1) for lag in range(1, FILT)
    ]


def filtered(shifted, taps_ref, branch, channel):
    total = shifted[0] * taps_ref[branch * FILT, channel]
    for lag in range(1, FILT):
        total = total + shifted[lag] * taps_ref[branch * FILT + lag, channel]
    return total


def strided(ref, start, count, step):
    return ref[pl.ds(start, count, stride=step), :]


def kernel_call(kernel, shapes, smem=(), scratch=(), count=0, mib=6):
    return pl.pallas_call(
        kernel,
        out_shape=shapes,
        in_specs=[SMEM if index in smem else VMEM for index in range(count)],
        out_specs=[VMEM] * len(shapes),
        scratch_shapes=list(scratch),
        compiler_params=pltpu.CompilerParams(vmem_limit_bytes=mib * 2**20),
    )


def f32(*dims):
    return jax.ShapeDtypeStruct(dims, F32)


def bf16(*dims):
    return jax.ShapeDtypeStruct(dims, BF16)


def pack_kernel(width, side_ref, k_ref, v_ref, filt_ref, out_ref):
    low_side = side_ref[0, 0] == 1
    for start in range(0, k_ref.shape[1], LANES):
        into = slice(start // width, (start + LANES) // width)
        for index, ref in enumerate((k_ref, v_ref, filt_ref)):
            block = ref[:, start : start + LANES].astype(F32).T
            if ref is filt_ref:
                block = block - jnp.where(low_side, block.astype(BF16).astype(F32), 0.0)
            out_ref[into, index * width : (index + 1) * width, :] = (
                block.astype(BF16).reshape(LANES // width, width, LANES)
            )


def shifted(values, lag):
    return values[lag : lag + LANES]


HALO = 8


def prepare_kernel(q_ref, halo_ref, grad_ref, taps_ref, gain_ref, q_short_ref, grad_z_ref):
    for start in range(0, q_ref.shape[1], LANES):
        lanes = slice(start, start + LANES)
        extended = jnp.concatenate([halo_ref[:, lanes], q_ref[:, lanes]], 0).astype(F32)
        total = jnp.zeros((LANES, LANES), F32)
        for lag in range(FILT):
            total = total + shifted(extended, HALO - lag) * taps_ref[lag : lag + 1, lanes]
        q_short_ref[lanes, :] = total.T
        grad_z_ref[lanes, :] = (grad_ref[:, lanes].astype(F32) * gain_ref[:, lanes]).T


def unpack_inputs(payload_ref, width, groups, k_ref, v_ref, filt_ref):
    rows = payload_ref.shape[0] // groups
    span = rows * width
    for index, ref in enumerate((k_ref, v_ref)):
        ref[...] = payload_ref[:, index * width : (index + 1) * width, :].astype(F32).reshape(groups * span, LANES)
    if filt_ref is not None:
        parts = payload_ref[:, 2 * width : 3 * width, :].astype(F32)
        filt_ref[...] = (parts[:rows] + parts[rows:]).reshape(span, LANES)
    return rows, span


def short_pair(k_ref, v_ref, taps_ref, place, rows, width, channel):
    k_short = filtered(lagged(strided(k_ref, place, rows, width)), taps_ref, 1, channel)
    v_short = filtered(lagged(strided(v_ref, place, rows, width)), taps_ref, 2, channel)
    return k_short, v_short


def conv_kernel(width, groups, payload_ref, taps_ref, first_ref, last_ref, twiddle_ref, inner_ref, outer_ref,
                conv_ref, k_ref, v_ref, filt_ref):
    rows, span = unpack_inputs(payload_ref, width, groups, k_ref, v_ref, filt_ref)
    for start in range(0, width, 2):
        blocks = []
        for channel in (start, start + 1):
            for group in range(groups):
                k_short, v_short = short_pair(k_ref, v_ref, taps_ref, group * span + channel, rows, width, channel)
                blocks.append(k_short * v_short)
        blocks += [strided(filt_ref, channel, rows, width) for channel in (start, start + 1)]
        spec = forward(blocks, first_ref, twiddle_ref, inner_ref)
        pairs = 2 * groups * rows
        products = []
        for side in range(2):
            for group in range(groups):
                block = (side * groups + group) * rows
                filt = pairs + side * rows
                products.append(times(spec[block : block + rows], spec[filt : filt + rows], False))
        convs = inverse(jnp.concatenate(products, 0), rows, last_ref, twiddle_ref, outer_ref)
        for side in range(2):
            for group in range(groups):
                conv_ref[pl.ds(group * span + start + side, rows, stride=width), :] = convs[side * groups + group]


def spectra_kernel(width, groups, payload_ref, taps_ref, first_ref, twiddle_ref, inner_ref,
                   out_ref, k_ref, v_ref, filt_ref):
    rows, span = unpack_inputs(payload_ref, width, groups, k_ref, v_ref, filt_ref)
    for start in range(0, width, 2):
        blocks = []
        for channel in (start, start + 1):
            for group in range(groups):
                k_short, v_short = short_pair(k_ref, v_ref, taps_ref, group * span + channel, rows, width, channel)
                below = (channel * groups + group) * rows + groups * span
                out_ref[below : below + rows, :LANES] = k_short
                out_ref[below : below + rows, LANES:] = v_short
                blocks.append(k_short * v_short)
        blocks += [strided(filt_ref, channel, rows, width) for channel in (start, start + 1)]
        spec = forward(blocks, first_ref, twiddle_ref, inner_ref)
        pairs = 2 * groups * rows
        out_ref[start * groups * rows : (start + 2) * groups * rows, :] = spec[:pairs]
        below = 2 * groups * span + start * rows
        out_ref[below : below + 2 * rows, :] = spec[pairs:]


def stats_kernel(conv_ref, q_short_ref, grad_z_ref, stats_ref):
    squares = jnp.zeros((LANES, LANES), F32)
    prods = squares
    for start in range(0, conv_ref.shape[0], LANES):
        lanes = slice(start, start + LANES)
        y_out = q_short_ref[lanes, :] * conv_ref[lanes, :]
        squares = squares + y_out * y_out
        prods = prods + grad_z_ref[lanes, :] * y_out
    squares = jnp.sum(squares, 0, keepdims=True)
    prods = jnp.sum(prods, 0, keepdims=True)
    for peer in range(stats_ref.shape[0]):
        stats_ref[peer, 0:1, :] = squares
        stats_ref[peer, 1:2, :] = prods


def scales(stats_ref):
    stats = jnp.sum(stats_ref[...], axis=0)
    rms = jnp.sqrt(stats[0:1] / D + EPS)
    return rms, stats[1:2] / (D * rms * rms * rms)


def dconv_kernel(conv_ref, q_short_ref, grad_z_ref, stats_ref, dconv_ref):
    rms, slope = scales(stats_ref)
    inverse_rms = 1.0 / rms
    for start in range(0, conv_ref.shape[0], LANES):
        lanes = slice(start, start + LANES)
        q_short = q_short_ref[lanes, :]
        y_out = q_short * conv_ref[lanes, :]
        dconv_ref[lanes, :] = (grad_z_ref[lanes, :] * inverse_rms - y_out * slope) * q_short


def norm_kernel(conv_ref, q_short_ref, grad_z_ref, stats_ref, q_ref, halo_ref, gain_ref,
                mixed_ref, grad_ref, edge_ref, short_ref):
    rms, slope = scales(stats_ref)
    inverse_rms = 1.0 / rms
    for start in range(0, conv_ref.shape[0], LANES):
        lanes = slice(start, start + LANES)
        conv = conv_ref[lanes, :]
        y_out = q_short_ref[lanes, :] * conv
        mixed_ref[:, lanes] = ((y_out / rms).T * gain_ref[:, lanes]).astype(BF16)
        grad = ((grad_z_ref[lanes, :] * inverse_rms - y_out * slope) * conv).T
        grad_ref[:, lanes] = grad
        edge_ref[:, lanes] = grad[:HALO]
        extended = jnp.concatenate([halo_ref[:, lanes], q_ref[:, lanes]], 0).astype(F32)
        for lag in range(FILT):
            short_ref[lag : lag + 1, lanes] = jnp.sum(grad * shifted(extended, HALO - lag), 0, keepdims=True)


def grad_q_kernel(grad_ref, edge_ref, taps_ref, out_ref):
    for start in range(0, grad_ref.shape[1], LANES):
        lanes = slice(start, start + LANES)
        extended = jnp.concatenate([grad_ref[:, lanes], edge_ref[:, lanes]], 0)
        total = jnp.zeros((LANES, LANES), F32)
        for lag in range(FILT):
            total = total + shifted(extended, lag) * taps_ref[lag : lag + 1, lanes]
        out_ref[:, lanes] = total.astype(BF16)


def back_kernel(width, groups, scale, dconv_ref, payload_ref, saved_ref, taps_ref, first_ref, last_ref,
                twiddle_ref, inner_ref, outer_ref, out_ref, k_ref, v_ref, grad_k_ref, grad_v_ref, dfilt_ref, short_ref):
    rows, span = unpack_inputs(payload_ref, width, groups, k_ref, v_ref, None)
    part_width = width // groups
    short_ref[...] = jnp.zeros(short_ref.shape, F32)
    dfilt_ref[...] = jnp.zeros(dfilt_ref.shape, F32)
    for start in range(0, width, 2):
        blocks = []
        for channel in (start, start + 1):
            for group in range(groups):
                blocks.append(strided(dconv_ref, group * span + channel, rows, width))
        spec = forward(blocks, first_ref, twiddle_ref, inner_ref)
        below = 2 * groups * span + start * rows
        spec_filt = saved_ref[below : below + 2 * rows, :]
        spec_kv = saved_ref[start * groups * rows : (start + 2) * groups * rows, :]
        products = []
        filters = []
        for side in range(2):
            total = 0.0
            for group in range(groups):
                block = (side * groups + group) * rows
                part = spec[block : block + rows]
                products.append(times(spec_filt[side * rows : (side + 1) * rows], part, True))
                total = total + times(spec_kv[block : block + rows], part, True)
            filters.append(total)
        results = inverse(jnp.concatenate(products + filters, 0), rows, last_ref, twiddle_ref, outer_ref)
        for side in range(2):
            channel = start + side
            target = channel // part_width * span + channel % part_width
            dfilt_ref[pl.ds(target, rows, stride=width), :] = results[2 * groups + side] * scale
            for group in range(groups):
                place = group * span + channel
                dkv = results[side * groups + group]
                k_lags = lagged(strided(k_ref, place, rows, width))
                v_lags = lagged(strided(v_ref, place, rows, width))
                below = (channel * groups + group) * rows + groups * span
                grad_k = dkv * saved_ref[below : below + rows, LANES:]
                grad_v = dkv * saved_ref[below : below + rows, :LANES]
                grad_k_ref[pl.ds(place, rows, stride=width), :] = filtered(led(grad_k), taps_ref, 1, channel)
                grad_v_ref[pl.ds(place, rows, stride=width), :] = filtered(led(grad_v), taps_ref, 2, channel)
                for branch, (grad, lags) in enumerate(((grad_k, k_lags), (grad_v, v_lags))):
                    for lag in range(FILT):
                        row = (branch * FILT + lag) * width + channel
                        short_ref[row : row + 1, :] += jnp.sum(grad * lags[lag], axis=0, keepdims=True)
    peers = groups * rows
    out_ref[:, :width, :] = grad_k_ref[...].reshape(peers, width, LANES).astype(BF16)
    out_ref[:, width : 2 * width, :] = grad_v_ref[...].reshape(peers, width, LANES).astype(BF16)
    short = jnp.sum(short_ref[...].T, axis=0, keepdims=True) * scale
    high = short.astype(BF16).astype(F32)
    for row, values in enumerate((high, short - high)):
        dfilt_ref[pl.ds(part_width + row, peers, stride=width), :] = jnp.broadcast_to(values, (peers, LANES))
    out_ref[:, 2 * width :, :] = dfilt_ref[...].reshape(peers, width, LANES).astype(BF16)


def part_kernel(width, part_width, payload_ref, part_ref, short_ref, rows_ref, out_ref):
    peers = payload_ref.shape[0]
    rows_ref[...] = payload_ref[:, 2 * width :, :].astype(F32).reshape(peers * width, LANES)
    for row in range(part_width):
        out_ref[pl.ds(row, peers, stride=part_width), :] = strided(rows_ref, row, peers, width)
    part_ref[...] = out_ref[...].astype(BF16)
    short_ref[...] = strided(rows_ref, part_width, peers, width) + strided(rows_ref, part_width + 1, peers, width)


def unpack_kernel(width, payload_ref, grad_q_ref, grads_ref):
    grads_ref[0, 0] = grad_q_ref[...]
    for start in range(0, grad_q_ref.shape[1], LANES):
        source = slice(start // width, (start + LANES) // width)
        for index in range(2):
            block = payload_ref[source, index * width : (index + 1) * width, :].astype(F32)
            grads_ref[1 + index, 0, :, start : start + LANES] = block.reshape(LANES, LANES).T.astype(BF16)


def join_kernel(width, part_width, side_ref, own_ref, other_ref, long_ref, from_ref, rows_ref):
    peers = long_ref.shape[1] // width
    for order, ref in ((side_ref[0, 0], own_ref), (1 - side_ref[0, 0], other_ref)):
        from_ref[...] = ref[...].astype(F32)
        for row in range(part_width):
            rows_ref[pl.ds(order * part_width + row, peers, stride=width), :] = strided(
                from_ref, row, peers, part_width
            )
    for start in range(0, long_ref.shape[1], LANES):
        long_ref[:, start : start + LANES] = rows_ref[start : start + LANES, :].T


def encode(values, top):
    root = jnp.sqrt(jnp.sqrt(jnp.abs(values))) * (60000.0 / top**0.25)
    return jnp.where(values < 0, -root, root).astype(jnp.float16)


def decode(code, top):
    root = code.astype(F32) * (top**0.25 / 60000.0)
    square = root * root
    return jnp.where(root < 0, -square * square, square * square)


PEERS = ("dp", "context")


def exchange(payload):
    return lax.all_to_all(payload, PEERS, split_axis=0, concat_axis=0, tiled=True)


def paired_sum(values, axis, bit):
    return values + lax.ppermute(values, axis, [(i, i ^ bit) for i in range(lax.axis_size(axis))])


def passed_along(values, by):
    size = lax.axis_size("context")
    pairs = [(i, i + by) for i in range(size) if 0 <= i + by < size]
    return lax.ppermute(values, "context", pairs)


def shards(q_in, k_in, v_in, short_filt, long_filt, norm_gain, grad_out):
    rows = lax.axis_size("context")
    groups = lax.axis_size("dp")
    peers = rows * groups
    channels = q_in.shape[2]
    width = channels // peers
    size = peers * width
    place = lax.axis_index(PEERS)
    first, last, twiddle, inner, outer = (jnp.asarray(t) for t in tables(rows))
    scratch = pltpu.VMEM((size, LANES), F32)
    scale = 1.0 / math.sqrt(groups * rows * LANES)
    gain = norm_gain[None]
    taps_q = jnp.pad(short_filt[0], ((0, 1), (0, 0)))
    taps = lax.dynamic_index_in_dim(short_filt.reshape(3 * FILT, peers, width), place, 1, keepdims=False)

    side = lax.axis_index("dp").astype(jnp.int32).reshape(1, 1)
    (payload,) = kernel_call(
        functools.partial(pack_kernel, width), [bf16(peers, 3 * width, LANES)], smem=(0,), count=4, mib=56
    )(side, k_in[0], v_in[0], long_filt)
    payload = exchange(payload)

    halo = passed_along(q_in[0, LANES - HALO :], 1)
    q_short, grad_z = kernel_call(prepare_kernel, [f32(channels, LANES)] * 2, count=5)(
        q_in[0], halo, grad_out[0], taps_q, gain
    )

    inputs = [scratch, scratch, pltpu.VMEM((rows * width, LANES), F32)]
    (conv,) = kernel_call(
        functools.partial(conv_kernel, width, groups),
        [f32(size, LANES)],
        smem=(1,),
        scratch=inputs,
        count=7,
        mib=10,
    )(payload, taps, first, last, twiddle, inner, outer)

    conv = exchange(encode(conv, 6.4e7).reshape(peers, width, LANES))
    conv = decode(conv, 6.4e7).reshape(size, LANES)
    (stats,) = kernel_call(stats_kernel, [f32(lax.axis_size("tensor"), 2, LANES)], count=3)(conv, q_short, grad_z)
    stats = lax.all_to_all(stats, "tensor", split_axis=0, concat_axis=0, tiled=True)
    (dconv,) = kernel_call(dconv_kernel, [f32(size, LANES)], count=4)(conv, q_short, grad_z, stats)
    dconv = exchange(encode(dconv, 4.6e8).reshape(peers, width, LANES))

    mixed, grad_0, edge, short_q = kernel_call(
        norm_kernel,
        [bf16(LANES, channels), f32(LANES, channels), f32(HALO, channels), f32(FILT, channels)],
        count=7,
    )(conv, q_short, grad_z, stats, q_in[0], halo, gain)
    edge = passed_along(edge, -1)
    (saved,) = kernel_call(
        functools.partial(spectra_kernel, width, groups),
        [f32(2 * size + rows * width, 2 * LANES)],
        smem=(1,),
        scratch=inputs,
        count=5,
        mib=10,
    )(payload, taps, first, twiddle, inner)
    bits = [1 << bit for bit in reversed(range(rows.bit_length() - 1))]
    early = len(bits) // 2
    for bit in bits[:early]:
        short_q = paired_sum(short_q, "context", bit)
    dconv, mixed, grad_0, edge, short_q, saved = lax.optimization_barrier(
        (dconv, mixed, grad_0, edge, short_q, saved)
    )
    dconv = decode(dconv, 4.6e8).reshape(size, LANES)
    (back,) = kernel_call(
        functools.partial(back_kernel, width, groups, scale),
        [bf16(peers, 3 * width, LANES)],
        smem=(3,),
        scratch=[scratch] * 5 + [pltpu.VMEM((LANES, LANES), F32)],
        count=9,
        mib=10,
    )(dconv, payload, saved, taps, first, last, twiddle, inner, outer)
    back = exchange(back)
    for bit in bits[early:]:
        short_q = paired_sum(short_q, "context", bit)
    for bit in range(groups.bit_length() - 1):
        short_q = paired_sum(short_q, "dp", 1 << bit)
    (grad_q,) = kernel_call(grad_q_kernel, [bf16(LANES, channels)], count=3)(grad_0, edge, taps_q)
    part_width = width // groups
    part_scratch = pltpu.VMEM((peers * part_width, LANES), F32)
    part, short = kernel_call(
        functools.partial(part_kernel, width, part_width),
        [bf16(peers * part_width, LANES), f32(peers, LANES)],
        scratch=[scratch, part_scratch],
        count=1,
    )(back)
    other = lax.ppermute(part, "dp", [(i, i ^ 1) for i in range(groups)])
    (grads,) = kernel_call(
        functools.partial(unpack_kernel, width), [bf16(3, 1, LANES, channels)], count=2
    )(back, grad_q)
    (grad_long,) = kernel_call(
        functools.partial(join_kernel, width, part_width),
        [f32(LANES, channels)],
        smem=(0,),
        scratch=[part_scratch, scratch],
        count=3,
    )(side, part, other)
    short = short[:, : 2 * FILT * width].reshape(peers, 2, FILT, width).transpose(1, 2, 0, 3)
    grad_short = jnp.concatenate([short_q[None] * scale, short.reshape(2, FILT, channels)])
    return (mixed[None], grads, grad_long, grad_short)


def solution(mesh):
    in_specs = (
        P("dp", "context", "tensor"),
        P("dp", "context", "tensor"),
        P("dp", "context", "tensor"),
        P(None, None, "tensor"),
        P("context", "tensor"),
        P("tensor"),
        P("dp", "context", "tensor"),
    )
    out_specs = (
        P("dp", "context", "tensor"),
        P(None, "dp", "context", "tensor"),
        P("context", "tensor"),
        P(None, None, "tensor"),
    )
    return jax.shard_map(shards, mesh=mesh, in_specs=in_specs, out_specs=out_specs, check_vma=False)
```

```python
import functools
import math

import jax
import jax.numpy as jnp
import numpy as np
from jax import lax
from jax.experimental import pallas as pl
from jax.experimental.pallas import tpu as pltpu
from jax.sharding import PartitionSpec as P

D = 4096
FILT = 7
EPS = 1e-06
LANES = 128
F32 = jnp.float32
BF16 = jnp.bfloat16
VMEM = pl.BlockSpec(memory_space=pltpu.VMEM)
SMEM = pl.BlockSpec(memory_space=pltpu.SMEM)


def halves(table):
    high = table.astype(jnp.bfloat16)
    low = (table - high.astype(np.float64)).astype(jnp.bfloat16)
    return high, low


@functools.cache
def tables(rows):
    size = rows * LANES
    row = np.arange(rows)
    lane = np.arange(LANES)
    angle = 2 * np.pi * np.outer(row + 0.25, row) / rows
    high, low = halves(np.concatenate([np.cos(angle), -np.sin(angle)], 0))
    first = np.concatenate([high, high, low], 1)
    high, low = halves(np.concatenate([np.cos(angle).T, -np.sin(angle).T], 1) / size)
    last = np.concatenate([high, high, low], 1)
    turn = 2 * np.pi * np.outer(row + 0.25, lane) / size
    twiddle = np.stack([np.cos(turn), -np.sin(turn)]).astype(np.float32)
    grid = 2 * np.pi * (np.outer(lane, lane) % LANES) / LANES
    cosine, sine = np.cos(grid), -np.sin(grid)
    high, low = halves(np.block([[cosine, sine], [-sine, cosine]]))
    inner = np.concatenate([high, high, low], 0)
    high, low = halves(np.block([[cosine, -sine], [sine, cosine]]))
    outer = np.concatenate([high, high, low], 0)
    return first, last, twiddle, inner, outer


def split(values):
    high = values.astype(BF16)
    return high, (values - high.astype(F32)).astype(BF16)


def dot(left, right):
    return jnp.dot(left, right, preferred_element_type=F32)


def forward(blocks, first_ref, twiddle_ref, inner_ref):
    rows = blocks[0].shape[0]
    real, imag = twiddle_ref[0], twiddle_ref[1]
    parts = []
    for pair in range(0, len(blocks), 2):
        high, low = split(jnp.concatenate(blocks[pair : pair + 2], 1))
        mixed = dot(first_ref[...], jnp.concatenate([high, low, high], 0))
        for side in range(2):
            lanes = slice(side * LANES, (side + 1) * LANES)
            re, im = mixed[:rows, lanes], mixed[rows:, lanes]
            parts.append(jnp.concatenate([re * real - im * imag, re * imag + im * real], 1))
    high, low = split(jnp.concatenate(parts, 0))
    return dot(jnp.concatenate([high, low, high], 1), inner_ref[...])


def inverse(spectra, rows, last_ref, twiddle_ref, outer_ref):
    real, imag = twiddle_ref[0], twiddle_ref[1]
    high, low = split(spectra)
    turned = dot(jnp.concatenate([high, low, high], 1), outer_ref[...])
    count = spectra.shape[0] // rows
    blocks = []
    for pair in range(0, count, 2):
        sides = []
        for block in (pair, pair + 1):
            re = turned[block * rows : (block + 1) * rows, :LANES]
            im = turned[block * rows : (block + 1) * rows, LANES:]
            sides.append(jnp.concatenate([re * real + im * imag, im * real - re * imag], 0))
        high, low = split(jnp.concatenate(sides, 1))
        out = dot(last_ref[...], jnp.concatenate([high, low, high], 0))
        blocks += [out[:, :LANES], out[:, LANES:]]
    return blocks


def times(left, right, conjugate):
    re_l, im_l = left[:, :LANES], left[:, LANES:]
    re_r, im_r = right[:, :LANES], right[:, LANES:]
    if conjugate:
        return jnp.concatenate([re_l * re_r + im_l * im_r, re_l * im_r - im_l * re_r], 1)
    return jnp.concatenate([re_l * re_r - im_l * im_r, re_l * im_r + im_l * re_r], 1)


def lagged(block):
    row = lax.broadcasted_iota(jnp.int32, block.shape, 0)
    lane = lax.broadcasted_iota(jnp.int32, block.shape, 1)
    above = jnp.where(row == 0, 0.0, pltpu.roll(block, 1, 0))
    return [block] + [
        pltpu.roll(jnp.where(lane >= LANES - lag, above, block), lag, 1) for lag in range(1, FILT)
    ]


def led(block):
    rows = block.shape[0]
    row = lax.broadcasted_iota(jnp.int32, block.shape, 0)
    lane = lax.broadcasted_iota(jnp.int32, block.shape, 1)
    below = jnp.where(row == rows - 1, 0.0, pltpu.roll(block, rows - 1, 0))
    return [block] + [
        pltpu.roll(jnp.where(lane < lag, below, block), LANES - lag, 1) for lag in range(1, FILT)
    ]


def filtered(shifted, taps_ref, branch, channel):
    total = shifted[0] * taps_ref[branch * FILT, channel]
    for lag in range(1, FILT):
        total = total + shifted[lag] * taps_ref[branch * FILT + lag, channel]
    return total


def strided(ref, start, count, step):
    return ref[pl.ds(start, count, stride=step), :]


def kernel_call(kernel, shapes, smem=(), scratch=(), count=0, mib=6):
    return pl.pallas_call(
        kernel,
        out_shape=shapes,
        in_specs=[SMEM if index in smem else VMEM for index in range(count)],
        out_specs=[VMEM] * len(shapes),
        scratch_shapes=list(scratch),
        compiler_params=pltpu.CompilerParams(vmem_limit_bytes=mib * 2**20),
    )


def f32(*dims):
    return jax.ShapeDtypeStruct(dims, F32)


def bf16(*dims):
    return jax.ShapeDtypeStruct(dims, BF16)


def pack_kernel(width, side_ref, k_ref, v_ref, filt_ref, out_ref):
    low_side = side_ref[0, 0] == 1
    for start in range(0, k_ref.shape[1], LANES):
        into = slice(start // width, (start + LANES) // width)
        for index, ref in enumerate((k_ref, v_ref, filt_ref)):
            block = ref[:, start : start + LANES].astype(F32).T
            if ref is filt_ref:
                block = block - jnp.where(low_side, block.astype(BF16).astype(F32), 0.0)
            out_ref[into, index * width : (index + 1) * width, :] = (
                block.astype(BF16).reshape(LANES // width, width, LANES)
            )


def shifted(values, lag):
    return values[lag : lag + LANES]


HALO = 8


def prepare_kernel(q_ref, halo_ref, grad_ref, taps_ref, gain_ref, q_short_ref, grad_z_ref):
    for start in range(0, q_ref.shape[1], LANES):
        lanes = slice(start, start + LANES)
        extended = jnp.concatenate([halo_ref[:, lanes], q_ref[:, lanes]], 0).astype(F32)
        total = jnp.zeros((LANES, LANES), F32)
        for lag in range(FILT):
            total = total + shifted(extended, HALO - lag) * taps_ref[lag : lag + 1, lanes]
        q_short_ref[lanes, :] = total.T
        grad_z_ref[lanes, :] = (grad_ref[:, lanes].astype(F32) * gain_ref[:, lanes]).T


def unpack_inputs(payload_ref, width, groups, k_ref, v_ref, filt_ref):
    rows = payload_ref.shape[0] // groups
    span = rows * width
    for index, ref in enumerate((k_ref, v_ref)):
        ref[...] = payload_ref[:, index * width : (index + 1) * width, :].astype(F32).reshape(groups * span, LANES)
    if filt_ref is not None:
        parts = payload_ref[:, 2 * width : 3 * width, :].astype(F32)
        filt_ref[...] = (parts[:rows] + parts[rows:]).reshape(span, LANES)
    return rows, span


def short_pair(k_ref, v_ref, taps_ref, place, rows, width, channel):
    k_short = filtered(lagged(strided(k_ref, place, rows, width)), taps_ref, 1, channel)
    v_short = filtered(lagged(strided(v_ref, place, rows, width)), taps_ref, 2, channel)
    return k_short, v_short


def conv_kernel(width, groups, payload_ref, taps_ref, first_ref, last_ref, twiddle_ref, inner_ref, outer_ref,
                conv_ref, k_ref, v_ref, filt_ref):
    rows, span = unpack_inputs(payload_ref, width, groups, k_ref, v_ref, filt_ref)
    for start in range(0, width, 2):
        blocks = []
        for channel in (start, start + 1):
            for group in range(groups):
                k_short, v_short = short_pair(k_ref, v_ref, taps_ref, group * span + channel, rows, width, channel)
                blocks.append(k_short * v_short)
        blocks += [strided(filt_ref, channel, rows, width) for channel in (start, start + 1)]
        spec = forward(blocks, first_ref, twiddle_ref, inner_ref)
        pairs = 2 * groups * rows
        products = []
        for side in range(2):
            for group in range(groups):
                block = (side * groups + group) * rows
                filt = pairs + side * rows
                products.append(times(spec[block : block + rows], spec[filt : filt + rows], False))
        convs = inverse(jnp.concatenate(products, 0), rows, last_ref, twiddle_ref, outer_ref)
        for side in range(2):
            for group in range(groups):
                conv_ref[pl.ds(group * span + start + side, rows, stride=width), :] = convs[side * groups + group]


def spectra_kernel(width, groups, payload_ref, taps_ref, first_ref, twiddle_ref, inner_ref,
                   out_ref, k_ref, v_ref, filt_ref):
    rows, span = unpack_inputs(payload_ref, width, groups, k_ref, v_ref, filt_ref)
    for start in range(0, width, 2):
        blocks = []
        for channel in (start, start + 1):
            for group in range(groups):
                k_short, v_short = short_pair(k_ref, v_ref, taps_ref, group * span + channel, rows, width, channel)
                below = (channel * groups + group) * rows + groups * span
                out_ref[below : below + rows, :LANES] = k_short
                out_ref[below : below + rows, LANES:] = v_short
                blocks.append(k_short * v_short)
        blocks += [strided(filt_ref, channel, rows, width) for channel in (start, start + 1)]
        spec = forward(blocks, first_ref, twiddle_ref, inner_ref)
        pairs = 2 * groups * rows
        out_ref[start * groups * rows : (start + 2) * groups * rows, :] = spec[:pairs]
        below = 2 * groups * span + start * rows
        out_ref[below : below + 2 * rows, :] = spec[pairs:]


def stats_kernel(conv_ref, q_short_ref, grad_z_ref, stats_ref):
    squares = jnp.zeros((LANES, LANES), F32)
    prods = squares
    for start in range(0, conv_ref.shape[0], LANES):
        lanes = slice(start, start + LANES)
        y_out = q_short_ref[lanes, :] * conv_ref[lanes, :]
        squares = squares + y_out * y_out
        prods = prods + grad_z_ref[lanes, :] * y_out
    squares = jnp.sum(squares, 0, keepdims=True)
    prods = jnp.sum(prods, 0, keepdims=True)
    for peer in range(stats_ref.shape[0]):
        stats_ref[peer, 0:1, :] = squares
        stats_ref[peer, 1:2, :] = prods


def scales(stats_ref):
    stats = jnp.sum(stats_ref[...], axis=0)
    rms = jnp.sqrt(stats[0:1] / D + EPS)
    return rms, stats[1:2] / (D * rms * rms * rms)


TAPS = 2 * HALO


def dconv_kernel(width, conv_ref, q_short_ref, grad_z_ref, stats_ref, q_ref, halo_ref,
                 dconv_ref, sums_ref, grad_ref, edge_ref, rows_ref):
    rms, slope = scales(stats_ref)
    inverse_rms = 1.0 / rms
    for start in range(0, conv_ref.shape[0], LANES):
        lanes = slice(start, start + LANES)
        q_short = q_short_ref[lanes, :]
        conv = conv_ref[lanes, :]
        grad_y = grad_z_ref[lanes, :] * inverse_rms - q_short * conv * slope
        dconv_ref[lanes, :] = grad_y * q_short
        grad = (grad_y * conv).T
        grad_ref[:, lanes] = grad
        edge_ref[:, lanes] = grad[:HALO]
        extended = jnp.concatenate([halo_ref[:, lanes], q_ref[:, lanes]], 0).astype(F32)
        sums = [
            jnp.sum(grad * shifted(extended, HALO - lag), 0, keepdims=True) for lag in range(FILT)
        ]
        rows_ref[lanes, :] = jnp.concatenate(sums + [jnp.zeros((LANES - FILT, LANES), F32)], 0).T
    peers = conv_ref.shape[0] // width
    total = strided(rows_ref, 0, peers, width)
    for channel in range(1, width):
        total = total + pltpu.roll(strided(rows_ref, channel, peers, width), channel * TAPS, 1)
    sums_ref[...] = total


def mixed_kernel(conv_ref, q_short_ref, stats_ref, gain_ref, mixed_ref):
    rms, _ = scales(stats_ref)
    for start in range(0, conv_ref.shape[0], LANES):
        lanes = slice(start, start + LANES)
        y_out = q_short_ref[lanes, :] * conv_ref[lanes, :]
        mixed_ref[:, lanes] = ((y_out / rms).T * gain_ref[:, lanes]).astype(BF16)


def grad_q_kernel(grad_ref, edge_ref, taps_ref, out_ref):
    for start in range(0, grad_ref.shape[1], LANES):
        lanes = slice(start, start + LANES)
        extended = jnp.concatenate([grad_ref[:, lanes], edge_ref[:, lanes]], 0)
        total = jnp.zeros((LANES, LANES), F32)
        for lag in range(FILT):
            total = total + shifted(extended, lag) * taps_ref[lag : lag + 1, lanes]
        out_ref[:, lanes] = total.astype(BF16)


def back_kernel(width, groups, scale, dconv_ref, sums_ref, payload_ref, saved_ref, taps_ref, first_ref, last_ref,
                twiddle_ref, inner_ref, outer_ref, out_ref, k_ref, v_ref, grad_k_ref, grad_v_ref, dfilt_ref, short_ref):
    rows, span = unpack_inputs(payload_ref, width, groups, k_ref, v_ref, None)
    part_width = width // groups
    short_ref[...] = jnp.zeros(short_ref.shape, F32)
    dfilt_ref[...] = jnp.zeros(dfilt_ref.shape, F32)
    for start in range(0, width, 2):
        blocks = []
        for channel in (start, start + 1):
            for group in range(groups):
                blocks.append(strided(dconv_ref, group * span + channel, rows, width))
        spec = forward(blocks, first_ref, twiddle_ref, inner_ref)
        below = 2 * groups * span + start * rows
        spec_filt = saved_ref[below : below + 2 * rows, :]
        spec_kv = saved_ref[start * groups * rows : (start + 2) * groups * rows, :]
        products = []
        filters = []
        for side in range(2):
            total = 0.0
            for group in range(groups):
                block = (side * groups + group) * rows
                part = spec[block : block + rows]
                products.append(times(spec_filt[side * rows : (side + 1) * rows], part, True))
                total = total + times(spec_kv[block : block + rows], part, True)
            filters.append(total)
        results = inverse(jnp.concatenate(products + filters, 0), rows, last_ref, twiddle_ref, outer_ref)
        for side in range(2):
            channel = start + side
            target = channel // part_width * span + channel % part_width
            dfilt_ref[pl.ds(target, rows, stride=width), :] = results[2 * groups + side] * scale
            for group in range(groups):
                place = group * span + channel
                dkv = results[side * groups + group]
                k_lags = lagged(strided(k_ref, place, rows, width))
                v_lags = lagged(strided(v_ref, place, rows, width))
                below = (channel * groups + group) * rows + groups * span
                grad_k = dkv * saved_ref[below : below + rows, LANES:]
                grad_v = dkv * saved_ref[below : below + rows, :LANES]
                grad_k_ref[pl.ds(place, rows, stride=width), :] = filtered(led(grad_k), taps_ref, 1, channel)
                grad_v_ref[pl.ds(place, rows, stride=width), :] = filtered(led(grad_v), taps_ref, 2, channel)
                for branch, (grad, lags) in enumerate(((grad_k, k_lags), (grad_v, v_lags))):
                    for lag in range(FILT):
                        row = channel * TAPS + branch * FILT + lag
                        short_ref[row : row + 1, :] += jnp.sum(grad * lags[lag], axis=0, keepdims=True)
    peers = groups * rows
    out_ref[:, :width, :] = grad_k_ref[...].reshape(peers, width, LANES).astype(BF16)
    out_ref[:, width : 2 * width, :] = grad_v_ref[...].reshape(peers, width, LANES).astype(BF16)
    short = (jnp.sum(short_ref[...].T, axis=0, keepdims=True), jnp.sum(sums_ref[...], axis=0, keepdims=True))
    for index, values in enumerate(short):
        values = values * scale
        high = values.astype(BF16).astype(F32)
        for row, part in enumerate((high, values - high)):
            start = part_width + 2 * index + row
            dfilt_ref[pl.ds(start, peers, stride=width), :] = jnp.broadcast_to(part, (peers, LANES))
    out_ref[:, 2 * width :, :] = dfilt_ref[...].reshape(peers, width, LANES).astype(BF16)


def part_kernel(width, part_width, payload_ref, part_ref, short_ref, rows_ref, out_ref):
    peers = payload_ref.shape[0]
    rows_ref[...] = payload_ref[:, 2 * width :, :].astype(F32).reshape(peers * width, LANES)
    for row in range(part_width):
        out_ref[pl.ds(row, peers, stride=part_width), :] = strided(rows_ref, row, peers, width)
    part_ref[...] = out_ref[...].astype(BF16)
    short_kv, short_q = (
        strided(rows_ref, start, peers, width) + strided(rows_ref, start + 1, peers, width)
        for start in (part_width, part_width + 2)
    )
    lane = lax.broadcasted_iota(jnp.int32, short_q.shape, 1)
    for channel in range(width):
        back = LANES - channel * TAPS
        rows_ref[pl.ds(channel, peers, stride=width), :] = jnp.where(
            lane < FILT, pltpu.roll(short_q, back % LANES, 1), pltpu.roll(short_kv, (back + FILT) % LANES, 1)
        )
    for start in range(0, short_ref.shape[2], LANES):
        block = rows_ref[start : start + LANES, :].T
        for branch in range(3):
            short_ref[branch, :, start : start + LANES] = block[branch * FILT : (branch + 1) * FILT]


def unpack_kernel(width, payload_ref, grad_q_ref, grads_ref):
    grads_ref[0, 0] = grad_q_ref[...]
    for start in range(0, grad_q_ref.shape[1], LANES):
        source = slice(start // width, (start + LANES) // width)
        for index in range(2):
            block = payload_ref[source, index * width : (index + 1) * width, :].astype(F32)
            grads_ref[1 + index, 0, :, start : start + LANES] = block.reshape(LANES, LANES).T.astype(BF16)


def join_kernel(width, part_width, side_ref, own_ref, other_ref, long_ref, from_ref, rows_ref):
    peers = long_ref.shape[1] // width
    for order, ref in ((side_ref[0, 0], own_ref), (1 - side_ref[0, 0], other_ref)):
        from_ref[...] = ref[...].astype(F32)
        for row in range(part_width):
            rows_ref[pl.ds(order * part_width + row, peers, stride=width), :] = strided(
                from_ref, row, peers, part_width
            )
    for start in range(0, long_ref.shape[1], LANES):
        long_ref[:, start : start + LANES] = rows_ref[start : start + LANES, :].T


def encode(values, top):
    root = jnp.sqrt(jnp.sqrt(jnp.abs(values))) * (60000.0 / top**0.25)
    return jnp.where(values < 0, -root, root).astype(jnp.float16)


def decode(code, top):
    root = code.astype(F32) * (top**0.25 / 60000.0)
    square = root * root
    return jnp.where(root < 0, -square * square, square * square)


PEERS = ("dp", "context")


def exchange(payload):
    return lax.all_to_all(payload, PEERS, split_axis=0, concat_axis=0, tiled=True)


def passed_along(values, by):
    size = lax.axis_size("context")
    pairs = [(i, i + by) for i in range(size) if 0 <= i + by < size]
    return lax.ppermute(values, "context", pairs)


def shards(q_in, k_in, v_in, short_filt, long_filt, norm_gain, grad_out):
    rows = lax.axis_size("context")
    groups = lax.axis_size("dp")
    peers = rows * groups
    channels = q_in.shape[2]
    width = channels // peers
    size = peers * width
    place = lax.axis_index(PEERS)
    first, last, twiddle, inner, outer = (jnp.asarray(t) for t in tables(rows))
    scratch = pltpu.VMEM((size, LANES), F32)
    scale = 1.0 / math.sqrt(groups * rows * LANES)
    gain = norm_gain[None]
    taps_q = jnp.pad(short_filt[0], ((0, 1), (0, 0)))
    taps = lax.dynamic_index_in_dim(short_filt.reshape(3 * FILT, peers, width), place, 1, keepdims=False)

    side = lax.axis_index("dp").astype(jnp.int32).reshape(1, 1)
    (payload,) = kernel_call(
        functools.partial(pack_kernel, width), [bf16(peers, 3 * width, LANES)], smem=(0,), count=4, mib=56
    )(side, k_in[0], v_in[0], long_filt)
    payload = exchange(payload)

    halo = passed_along(q_in[0, LANES - HALO :], 1)
    q_short, grad_z = kernel_call(prepare_kernel, [f32(channels, LANES)] * 2, count=5)(
        q_in[0], halo, grad_out[0], taps_q, gain
    )

    inputs = [scratch, scratch, pltpu.VMEM((rows * width, LANES), F32)]
    (conv,) = kernel_call(
        functools.partial(conv_kernel, width, groups),
        [f32(size, LANES)],
        smem=(1,),
        scratch=inputs,
        count=7,
        mib=10,
    )(payload, taps, first, last, twiddle, inner, outer)

    conv = exchange(encode(conv, 6.4e7).reshape(peers, width, LANES))
    conv = decode(conv, 6.4e7).reshape(size, LANES)
    (stats,) = kernel_call(stats_kernel, [f32(lax.axis_size("tensor"), 2, LANES)], count=3)(conv, q_short, grad_z)
    stats = lax.all_to_all(stats, "tensor", split_axis=0, concat_axis=0, tiled=True)
    dconv, sums, grad_0, edge = kernel_call(
        functools.partial(dconv_kernel, width),
        [f32(size, LANES), f32(peers, LANES), f32(LANES, channels), f32(HALO, channels)],
        scratch=[scratch],
        count=6,
    )(conv, q_short, grad_z, stats, q_in[0], halo)
    code = encode(dconv, 4.6e8).reshape(peers, width // 2, 2, LANES)
    sums = jnp.pad(encode(sums, 1e18).reshape(peers, 1, 1, LANES), ((0, 0), (0, 0), (0, 1), (0, 0)))
    code = exchange(jnp.concatenate([code, sums], 1))

    edge = passed_along(edge, -1)
    (mixed,) = kernel_call(mixed_kernel, [bf16(LANES, channels)], count=4)(conv, q_short, stats, gain)
    (grad_q,) = kernel_call(grad_q_kernel, [bf16(LANES, channels)], count=3)(grad_0, edge, taps_q)
    (saved,) = kernel_call(
        functools.partial(spectra_kernel, width, groups),
        [f32(2 * size + rows * width, 2 * LANES)],
        smem=(1,),
        scratch=inputs,
        count=5,
        mib=10,
    )(payload, taps, first, twiddle, inner)
    code, mixed, grad_q, saved = lax.optimization_barrier((code, mixed, grad_q, saved))

    dconv = decode(code[:, : width // 2], 4.6e8).reshape(size, LANES)
    sums = decode(code[:, width // 2, 0], 1e18)
    (back,) = kernel_call(
        functools.partial(back_kernel, width, groups, scale),
        [bf16(peers, 3 * width, LANES)],
        smem=(4,),
        scratch=[scratch] * 5 + [pltpu.VMEM((LANES, LANES), F32)],
        count=10,
        mib=10,
    )(dconv, sums, payload, saved, taps, first, last, twiddle, inner, outer)
    back = exchange(back)
    part_width = width // groups
    part_scratch = pltpu.VMEM((peers * part_width, LANES), F32)
    part, grad_short = kernel_call(
        functools.partial(part_kernel, width, part_width),
        [bf16(peers * part_width, LANES), f32(3, FILT, channels)],
        scratch=[scratch, part_scratch],
        count=1,
    )(back)
    other = lax.ppermute(part, "dp", [(i, i ^ 1) for i in range(groups)])
    (grads,) = kernel_call(
        functools.partial(unpack_kernel, width), [bf16(3, 1, LANES, channels)], count=2
    )(back, grad_q)
    (grad_long,) = kernel_call(
        functools.partial(join_kernel, width, part_width),
        [f32(LANES, channels)],
        smem=(0,),
        scratch=[part_scratch, scratch],
        count=3,
    )(side, part, other)
    return (mixed[None], grads, grad_long, grad_short)


def solution(mesh):
    in_specs = (
        P("dp", "context", "tensor"),
        P("dp", "context", "tensor"),
        P("dp", "context", "tensor"),
        P(None, None, "tensor"),
        P("context", "tensor"),
        P("tensor"),
        P("dp", "context", "tensor"),
    )
    out_specs = (
        P("dp", "context", "tensor"),
        P(None, "dp", "context", "tensor"),
        P("context", "tensor"),
        P(None, None, "tensor"),
    )
    return jax.shard_map(shards, mesh=mesh, in_specs=in_specs, out_specs=out_specs, check_vma=False)
```

```python
import functools
import math

import jax
import jax.numpy as jnp
import numpy as np
from jax import lax
from jax.experimental import pallas as pl
from jax.experimental.pallas import tpu as pltpu
from jax.sharding import PartitionSpec as P

D = 4096
FILT = 7
EPS = 1e-06
LANES = 128
F32 = jnp.float32
BF16 = jnp.bfloat16
VMEM = pl.BlockSpec(memory_space=pltpu.VMEM)
SMEM = pl.BlockSpec(memory_space=pltpu.SMEM)


def halves(table):
    high = table.astype(jnp.bfloat16)
    low = (table - high.astype(np.float64)).astype(jnp.bfloat16)
    return high, low


@functools.cache
def tables(rows):
    size = rows * LANES
    row = np.arange(rows)
    lane = np.arange(LANES)
    angle = 2 * np.pi * np.outer(row + 0.25, row) / rows
    high, low = halves(np.concatenate([np.cos(angle), -np.sin(angle)], 0))
    first = np.concatenate([high, high, low], 1)
    high, low = halves(np.concatenate([np.cos(angle).T, np.sin(angle).T], 1) / size)
    last = np.concatenate([high, high, low], 1)
    turn = 2 * np.pi * np.outer(row + 0.25, lane) / size
    twiddle = np.concatenate([np.cos(turn), -np.sin(turn)], 1)
    twiddles = []
    for _ in range(3):
        twiddles.append(twiddle.astype(jnp.bfloat16))
        twiddle = twiddle - twiddles[-1].astype(np.float64)
    grid = 2 * np.pi * (np.outer(lane, lane) % LANES) / LANES
    cosine, sine = np.cos(grid), -np.sin(grid)
    inner = np.concatenate(halves(np.block([[cosine, sine], [-sine, cosine]])), 0)
    wide = lambda part: np.pad(part, ((0, 0), (0, 2 * LANES - part.shape[1])))
    return np.concatenate([inner, wide(first), wide(last[:, : 2 * LANES]), wide(last[:, 2 * LANES :])] + twiddles, 0)


class Tables:
    def __init__(self, ref, rows):
        self.ref, self.rows = ref, rows
        start = 4 * LANES + 4 * rows
        parts = [ref[start + index * rows : start + (index + 1) * rows, :].astype(F32) for index in range(3)]
        twiddle = parts[0] + parts[1] + parts[2]
        self.real, self.imag = twiddle[:, :LANES], twiddle[:, LANES:]

    def inner(self):
        high, low = self.ref[: 2 * LANES, :], self.ref[2 * LANES : 4 * LANES, :]
        return jnp.concatenate([high, high, low], 0)

    def first(self):
        return self.ref[4 * LANES : 4 * LANES + 2 * self.rows, : 3 * self.rows]

    def last(self):
        start, wide = 4 * LANES + 2 * self.rows, 6 * self.rows
        left = self.ref[start : start + self.rows, : min(wide, 2 * LANES)]
        if wide <= 2 * LANES:
            return left
        return jnp.concatenate([left, self.ref[start + self.rows : start + 2 * self.rows, : wide - 2 * LANES]], 1)

    def turned(self, real, imag):
        return real * self.real - imag * self.imag, real * self.imag + imag * self.real


def split(values):
    high = values.astype(BF16)
    return high, (values - high.astype(F32)).astype(BF16)


def dot(left, right):
    return jnp.dot(left, right, preferred_element_type=F32)


def along_lanes(values, table):
    high, low = split(values)
    return dot(jnp.concatenate([high, low, high], 1), table.inner())


def forward(blocks, table):
    rows = blocks[0].shape[0]
    parts = []
    for pair in range(0, len(blocks), 2):
        high, low = split(jnp.concatenate(blocks[pair : pair + 2], 1))
        mixed = dot(table.first(), jnp.concatenate([high, low, high], 0))
        for side in range(2):
            lanes = slice(side * LANES, (side + 1) * LANES)
            parts.append(jnp.concatenate(table.turned(mixed[:rows, lanes], mixed[rows:, lanes]), 1))
    return along_lanes(jnp.concatenate(parts, 0), table)


def inverse(conjugates, rows, table):
    values = along_lanes(conjugates, table)
    count = conjugates.shape[0] // rows
    blocks = []
    for pair in range(0, count, 2):
        sides = []
        for block in (pair, pair + 1):
            part = values[block * rows : (block + 1) * rows]
            sides.append(jnp.concatenate(table.turned(part[:, :LANES], part[:, LANES:]), 0))
        high, low = split(jnp.concatenate(sides, 1))
        out = dot(table.last(), jnp.concatenate([high, low, high], 0))
        blocks += [out[:, :LANES], out[:, LANES:]]
    return blocks


def times(left, right, conjugate):
    re_l, im_l = left[:, :LANES], left[:, LANES:]
    re_r, im_r = right[:, :LANES], right[:, LANES:]
    if conjugate:
        return jnp.concatenate([re_l * re_r + im_l * im_r, im_l * re_r - re_l * im_r], 1)
    return jnp.concatenate([re_l * re_r - im_l * im_r, -(re_l * im_r + im_l * re_r)], 1)


def lagged(values):
    above, block = values[:-1], values[1:]
    lane = lax.broadcasted_iota(jnp.int32, block.shape, 2)
    return [block] + [
        pltpu.roll(jnp.where(lane >= LANES - lag, above, block), lag, 2) for lag in range(1, FILT)
    ]


def led(values):
    block, below = values[:-1], values[1:]
    lane = lax.broadcasted_iota(jnp.int32, block.shape, 2)
    return [block] + [
        pltpu.roll(jnp.where(lane < lag, below, block), LANES - lag, 2) for lag in range(1, FILT)
    ]


def filtered(shifted, taps_ref, branch):
    total = shifted[0] * taps_ref[branch * FILT][None]
    for lag in range(1, FILT):
        total = total + shifted[lag] * taps_ref[branch * FILT + lag][None]
    return total


def strided(ref, start, count, step):
    return ref[pl.ds(start, count, stride=step), :]


def kernel_call(kernel, shapes, smem=(), scratch=(), count=0, mib=6):
    return pl.pallas_call(
        kernel,
        out_shape=shapes,
        in_specs=[SMEM if index in smem else VMEM for index in range(count)],
        out_specs=[VMEM] * len(shapes),
        scratch_shapes=list(scratch),
        compiler_params=pltpu.CompilerParams(vmem_limit_bytes=mib * 2**20),
    )


def f32(*dims):
    return jax.ShapeDtypeStruct(dims, F32)


def bf16(*dims):
    return jax.ShapeDtypeStruct(dims, BF16)


def pack_kernel(width, side_ref, k_ref, v_ref, filt_ref, out_ref):
    low_side = side_ref[0, 0] == 1
    for start in range(0, k_ref.shape[1], LANES):
        into = slice(start // width, (start + LANES) // width)
        for index, ref in enumerate((k_ref, v_ref, filt_ref)):
            block = ref[:, start : start + LANES].astype(F32).T
            if ref is filt_ref:
                block = block - jnp.where(low_side, block.astype(BF16).astype(F32), 0.0)
            out_ref[into, index * width : (index + 1) * width, :] = (
                block.astype(BF16).reshape(LANES // width, width, LANES)
            )


def shifted(values, lag):
    return values[lag : lag + LANES]


HALO = 8


def prepare_kernel(q_ref, halo_ref, grad_ref, taps_ref, gain_ref, q_short_ref, grad_z_ref):
    for start in range(0, q_ref.shape[1], LANES):
        lanes = slice(start, start + LANES)
        extended = jnp.concatenate([halo_ref[:, lanes], q_ref[:, lanes]], 0).astype(F32)
        total = jnp.zeros((LANES, LANES), F32)
        for lag in range(FILT):
            total = total + shifted(extended, HALO - lag) * taps_ref[lag : lag + 1, lanes]
        q_short_ref[lanes, :] = total.T
        grad_z_ref[lanes, :] = (grad_ref[:, lanes].astype(F32) * gain_ref[:, lanes]).T


STEP = 4
CHUNK = 8


def chunks(peers, groups):
    rows = peers // groups
    size = min(CHUNK, rows)
    for start in range(0, peers, size):
        yield start, size, start % rows == 0, (start + size) % rows == 0


def loaded(payload_ref, index, width, start, size, at_first):
    rows = slice(index * width, (index + 1) * width)
    if at_first:
        block = payload_ref[start : start + size, rows, :].astype(F32)
        return jnp.concatenate([jnp.zeros((1, width, LANES), F32), block], 0)
    return payload_ref[start - 1 : start + size, rows, :].astype(F32)


def make_inputs(payload_ref, taps_ref, width, groups, kv_ref, filt_ref):
    peers = payload_ref.shape[0]
    rows = peers // groups
    span = rows * width
    for start, size, at_first, _ in chunks(peers, groups):
        k_short = filtered(lagged(loaded(payload_ref, 0, width, start, size, at_first)), taps_ref, 1)
        v_short = filtered(lagged(loaded(payload_ref, 1, width, start, size, at_first)), taps_ref, 2)
        kv_ref[start * width : (start + size) * width, :] = (k_short * v_short).reshape(size * width, LANES)
    parts = payload_ref[:, 2 * width : 3 * width, :].astype(F32)
    filt_ref[...] = (parts[:rows] + parts[rows:]).reshape(span, LANES)
    return rows, span


def input_blocks(start, width, groups, rows, kv_ref, filt_ref):
    span = rows * width
    channels = range(start, start + STEP)
    blocks = [
        strided(kv_ref, group * span + channel, rows, width) for channel in channels for group in range(groups)
    ]
    return blocks + [strided(filt_ref, channel, rows, width) for channel in channels]


def conv_kernel(width, groups, payload_ref, taps_ref, table_ref,
                conv_ref, kv_ref, filt_ref):
    rows, span = make_inputs(payload_ref, taps_ref, width, groups, kv_ref, filt_ref)
    pairs = STEP * groups * rows
    table = Tables(table_ref, rows)
    for start in range(0, width, STEP):
        spec = forward(input_blocks(start, width, groups, rows, kv_ref, filt_ref), table)
        products = []
        for side in range(STEP):
            for group in range(groups):
                block = (side * groups + group) * rows
                filt = pairs + side * rows
                products.append(times(spec[block : block + rows], spec[filt : filt + rows], False))
        convs = inverse(jnp.concatenate(products, 0), rows, table)
        for side in range(STEP):
            for group in range(groups):
                conv_ref[pl.ds(group * span + start + side, rows, stride=width), :] = convs[side * groups + group]


def spectra_kernel(width, groups, payload_ref, taps_ref, table_ref, out_ref, kv_ref, filt_ref):
    rows, span = make_inputs(payload_ref, taps_ref, width, groups, kv_ref, filt_ref)
    pairs = STEP * groups * rows
    table = Tables(table_ref, rows)
    for start in range(0, width, STEP):
        spec = forward(input_blocks(start, width, groups, rows, kv_ref, filt_ref), table)
        out_ref[start * groups * rows : start * groups * rows + pairs, :] = spec[:pairs]
        below = groups * span + start * rows
        out_ref[below : below + STEP * rows, :] = spec[pairs:]


def stats_kernel(conv_ref, q_short_ref, grad_z_ref, stats_ref):
    squares = jnp.zeros((LANES, LANES), F32)
    prods = squares
    for start in range(0, conv_ref.shape[0], LANES):
        lanes = slice(start, start + LANES)
        y_out = q_short_ref[lanes, :] * conv_ref[lanes, :]
        squares = squares + y_out * y_out
        prods = prods + grad_z_ref[lanes, :] * y_out
    squares = jnp.sum(squares, 0, keepdims=True)
    prods = jnp.sum(prods, 0, keepdims=True)
    for peer in range(stats_ref.shape[0]):
        stats_ref[peer, 0:1, :] = squares
        stats_ref[peer, 1:2, :] = prods


def scales(stats_ref):
    stats = jnp.sum(stats_ref[...], axis=0)
    rms = jnp.sqrt(stats[0:1] / D + EPS)
    return rms, stats[1:2] / (D * rms * rms * rms)


TAPS = 2 * HALO
EXTRA = 2
SUMS_TOP = 1e18
CONV_TOP = 6.4e7
DCONV_TOP = 4.6e8


def dconv_kernel(width, conv_ref, q_short_ref, grad_z_ref, stats_ref, q_ref, halo_ref, out_ref, edge_ref, rows_ref):
    rms, slope = scales(stats_ref)
    inverse_rms = 1.0 / rms
    pitch = width + EXTRA
    for start in range(0, conv_ref.shape[0], LANES):
        lanes = slice(start, start + LANES)
        q_short = q_short_ref[lanes, :]
        conv = conv_ref[lanes, :]
        grad_y = grad_z_ref[lanes, :] * inverse_rms - q_short * conv * slope
        dconv = grad_y * q_short
        for peer in range(LANES // width):
            into = (start // width + peer) * pitch
            out_ref[into : into + width, :] = dconv[peer * width : (peer + 1) * width]
        grad = (grad_y * conv).T
        edge_ref[:, lanes] = grad[:HALO]
        extended = jnp.concatenate([halo_ref[:, lanes], q_ref[:, lanes]], 0).astype(F32)
        sums = [
            jnp.sum(grad * shifted(extended, HALO - lag), 0, keepdims=True) for lag in range(FILT)
        ]
        rows_ref[lanes, :] = jnp.concatenate(sums + [jnp.zeros((LANES - FILT, LANES), F32)], 0).T
    peers = conv_ref.shape[0] // width
    total = strided(rows_ref, 0, peers, width)
    for channel in range(1, width):
        total = total + pltpu.roll(strided(rows_ref, channel, peers, width), channel * TAPS, 1)
    out_ref[pl.ds(width, peers, stride=pitch), :] = total * (DCONV_TOP / SUMS_TOP)
    out_ref[pl.ds(width + 1, peers, stride=pitch), :] = jnp.zeros_like(total)


def mixed_kernel(conv_ref, q_short_ref, stats_ref, gain_ref, mixed_ref):
    rms, _ = scales(stats_ref)
    for start in range(0, conv_ref.shape[0], LANES):
        lanes = slice(start, start + LANES)
        y_out = q_short_ref[lanes, :] * conv_ref[lanes, :]
        mixed_ref[:, lanes] = ((y_out / rms).T * gain_ref[:, lanes]).astype(BF16)


def grad_q_kernel(conv_ref, q_short_ref, grad_z_ref, stats_ref, edge_ref, taps_ref, out_ref):
    rms, slope = scales(stats_ref)
    inverse_rms = 1.0 / rms
    for start in range(0, conv_ref.shape[0], LANES):
        lanes = slice(start, start + LANES)
        conv = conv_ref[lanes, :]
        grad = (grad_z_ref[lanes, :] * inverse_rms - q_short_ref[lanes, :] * conv * slope) * conv
        extended = jnp.concatenate([grad.T, edge_ref[:, lanes]], 0)
        total = jnp.zeros((LANES, LANES), F32)
        for lag in range(FILT):
            total = total + shifted(extended, lag) * taps_ref[lag : lag + 1, lanes]
        out_ref[:, lanes] = total.astype(BF16)


def back_kernel(width, groups, scale, dconv_ref, payload_ref, saved_ref, taps_ref, table_ref, out_ref, dkv_ref, grad_k_ref, grad_v_ref, dfilt_ref, short_ref):
    peers = payload_ref.shape[0]
    rows = peers // groups
    span = rows * width
    part_width = width // groups
    pitch = width + EXTRA
    dfilt_ref[...] = jnp.zeros(dfilt_ref.shape, F32)
    table = Tables(table_ref, rows)
    for start in range(0, width, STEP):
        blocks = []
        for channel in range(start, start + STEP):
            for group in range(groups):
                blocks.append(strided(dconv_ref, group * rows * pitch + channel, rows, pitch))
        spec = forward(blocks, table)
        below = groups * span + start * rows
        spec_filt = saved_ref[below : below + STEP * rows, :]
        spec_kv = saved_ref[start * groups * rows : (start + STEP) * groups * rows, :]
        products = []
        filters = []
        for side in range(STEP):
            total = 0.0
            for group in range(groups):
                block = (side * groups + group) * rows
                part = spec[block : block + rows]
                products.append(times(spec_filt[side * rows : (side + 1) * rows], part, True))
                total = total + times(spec_kv[block : block + rows], part, True)
            filters.append(total)
        results = inverse(jnp.concatenate(products + filters, 0), rows, table)
        for side in range(STEP):
            channel = start + side
            target = channel // part_width * span + channel % part_width
            dfilt_ref[pl.ds(target, rows, stride=width), :] = results[STEP * groups + side] * scale
            for group in range(groups):
                place = group * span + channel
                dkv_ref[pl.ds(place, rows, stride=width), :] = results[side * groups + group]
    totals = [0.0] * (2 * FILT)
    for start, size, at_first, _ in chunks(peers, groups):
        into = slice(start * width, (start + size) * width)
        dkv = dkv_ref[into, :].reshape(size, width, LANES)
        k_lags = lagged(loaded(payload_ref, 0, width, start, size, at_first))
        v_lags = lagged(loaded(payload_ref, 1, width, start, size, at_first))
        grad_k = dkv * filtered(v_lags, taps_ref, 2)
        grad_v = dkv * filtered(k_lags, taps_ref, 1)
        grad_k_ref[into, :] = grad_k.reshape(size * width, LANES)
        grad_v_ref[into, :] = grad_v.reshape(size * width, LANES)
        for branch, (grad, lags) in enumerate(((grad_k, k_lags), (grad_v, v_lags))):
            for lag in range(FILT):
                totals[branch * FILT + lag] = totals[branch * FILT + lag] + jnp.sum(grad * lags[lag], axis=0)
    for start, size, _, at_last in chunks(peers, groups):
        for index, ref in enumerate((grad_k_ref, grad_v_ref)):
            if at_last:
                values = ref[start * width : (start + size) * width, :]
                values = jnp.concatenate([values, jnp.zeros((width, LANES), F32)], 0)
            else:
                values = ref[start * width : (start + size + 1) * width, :]
            grads = filtered(led(values.reshape(size + 1, width, LANES)), taps_ref, 1 + index)
            out_ref[start : start + size, index * width : (index + 1) * width, :] = grads.astype(BF16)
    short_ref[...] = jnp.zeros(short_ref.shape, F32)
    for tap, total in enumerate(totals):
        short_ref[pl.ds(tap, width, stride=TAPS), :] = total
    sums = strided(dconv_ref, width, peers, pitch) * (SUMS_TOP / DCONV_TOP)
    short = (jnp.sum(short_ref[...].T, axis=0, keepdims=True), jnp.sum(sums, axis=0, keepdims=True))
    for index, values in enumerate(short):
        values = values * scale
        high = values.astype(BF16).astype(F32)
        for row, part in enumerate((high, values - high)):
            start = part_width + 2 * index + row
            dfilt_ref[pl.ds(start, peers, stride=width), :] = jnp.broadcast_to(part, (peers, LANES))
    out_ref[:, 2 * width :, :] = dfilt_ref[...].reshape(peers, width, LANES).astype(BF16)


def part_kernel(width, part_width, payload_ref, part_ref, short_ref, rows_ref, out_ref):
    peers = payload_ref.shape[0]
    rows_ref[...] = payload_ref[:, 2 * width :, :].astype(F32).reshape(peers * width, LANES)
    for row in range(part_width):
        out_ref[pl.ds(row, peers, stride=part_width), :] = strided(rows_ref, row, peers, width)
    part_ref[...] = out_ref[...].astype(BF16)
    short_kv, short_q = (
        strided(rows_ref, start, peers, width) + strided(rows_ref, start + 1, peers, width)
        for start in (part_width, part_width + 2)
    )
    lane = lax.broadcasted_iota(jnp.int32, short_q.shape, 1)
    for channel in range(width):
        back = LANES - channel * TAPS
        rows_ref[pl.ds(channel, peers, stride=width), :] = jnp.where(
            lane < FILT, pltpu.roll(short_q, back % LANES, 1), pltpu.roll(short_kv, (back + FILT) % LANES, 1)
        )
    for start in range(0, short_ref.shape[2], LANES):
        block = rows_ref[start : start + LANES, :].T
        for branch in range(3):
            short_ref[branch, :, start : start + LANES] = block[branch * FILT : (branch + 1) * FILT]


def unpack_kernel(width, payload_ref, grad_q_ref, grads_ref):
    grads_ref[0, 0] = grad_q_ref[...]
    for start in range(0, grad_q_ref.shape[1], LANES):
        source = slice(start // width, (start + LANES) // width)
        for index in range(2):
            block = payload_ref[source, index * width : (index + 1) * width, :].astype(F32)
            grads_ref[1 + index, 0, :, start : start + LANES] = block.reshape(LANES, LANES).T.astype(BF16)


def join_kernel(width, part_width, side_ref, own_ref, other_ref, long_ref, from_ref, rows_ref):
    peers = long_ref.shape[1] // width
    for order, ref in ((side_ref[0, 0], own_ref), (1 - side_ref[0, 0], other_ref)):
        from_ref[...] = ref[...].astype(F32)
        for row in range(part_width):
            rows_ref[pl.ds(order * part_width + row, peers, stride=width), :] = strided(
                from_ref, row, peers, part_width
            )
    for start in range(0, long_ref.shape[1], LANES):
        long_ref[:, start : start + LANES] = rows_ref[start : start + LANES, :].T


def encode(values, top):
    root = lax.rsqrt(lax.rsqrt(jnp.abs(values))) * (60000.0 / top**0.25)
    return jnp.where(values < 0, -root, root).astype(jnp.float16)


def decode(code, top):
    root = code.astype(F32) * (top**0.25 / 60000.0)
    square = root * root
    return jnp.where(root < 0, -square * square, square * square)


PEERS = ("dp", "context")


def exchange(payload):
    return lax.all_to_all(payload, PEERS, split_axis=0, concat_axis=0, tiled=True)


def passed_along(values, by):
    size = lax.axis_size("context")
    pairs = [(i, i + by) for i in range(size) if 0 <= i + by < size]
    return lax.ppermute(values, "context", pairs)


def shards(q_in, k_in, v_in, short_filt, long_filt, norm_gain, grad_out):
    rows = lax.axis_size("context")
    groups = lax.axis_size("dp")
    peers = rows * groups
    channels = q_in.shape[2]
    width = channels // peers
    size = peers * width
    place = lax.axis_index(PEERS)
    table = jnp.asarray(tables(rows))
    scratch = pltpu.VMEM((size, LANES), F32)
    scale = 1.0 / math.sqrt(groups * rows * LANES)
    gain = norm_gain[None]
    taps_q = jnp.pad(short_filt[0], ((0, 1), (0, 0)))
    taps = lax.dynamic_index_in_dim(short_filt.reshape(3 * FILT, peers, width), place, 1, keepdims=False)
    taps = jnp.broadcast_to(taps[:, :, None], (3 * FILT, width, LANES))

    side = lax.axis_index("dp").astype(jnp.int32).reshape(1, 1)
    (payload,) = kernel_call(
        functools.partial(pack_kernel, width), [bf16(peers, 3 * width, LANES)], smem=(0,), count=4, mib=56
    )(side, k_in[0], v_in[0], long_filt)
    payload = exchange(payload)

    halo = passed_along(q_in[0, LANES - HALO :], 1)
    q_short, grad_z = kernel_call(prepare_kernel, [f32(channels, LANES)] * 2, count=5)(
        q_in[0], halo, grad_out[0], taps_q, gain
    )

    inputs = [scratch, pltpu.VMEM((rows * width, LANES), F32)]
    (conv,) = kernel_call(
        functools.partial(conv_kernel, width, groups),
        [f32(size, LANES)],
        scratch=inputs,
        count=3,
        mib=10,
    )(payload, taps, table)

    conv = exchange(encode(conv, CONV_TOP).reshape(peers, width, LANES))
    conv = decode(conv, CONV_TOP).reshape(size, LANES)
    (stats,) = kernel_call(stats_kernel, [f32(lax.axis_size("tensor"), 2, LANES)], count=3)(conv, q_short, grad_z)
    stats = lax.all_to_all(stats, "tensor", split_axis=0, concat_axis=0, tiled=True)
    pitch = width + EXTRA
    dconv, edge = kernel_call(
        functools.partial(dconv_kernel, width),
        [f32(peers * pitch, LANES), f32(HALO, channels)],
        scratch=[scratch],
        count=6,
    )(conv, q_short, grad_z, stats, q_in[0], halo)
    code = exchange(encode(dconv, DCONV_TOP).reshape(peers, pitch // 2, 2, LANES))

    edge = passed_along(edge, -1)
    (mixed,) = kernel_call(mixed_kernel, [bf16(LANES, channels)], count=4)(conv, q_short, stats, gain)
    (grad_q,) = kernel_call(grad_q_kernel, [bf16(LANES, channels)], count=6)(
        conv, q_short, grad_z, stats, edge, taps_q
    )
    (saved,) = kernel_call(
        functools.partial(spectra_kernel, width, groups),
        [f32(size + rows * width, 2 * LANES)],
        scratch=inputs,
        count=3,
        mib=10,
    )(payload, taps, table)
    code, mixed, grad_q, saved = lax.optimization_barrier((code, mixed, grad_q, saved))

    dconv = decode(code, DCONV_TOP).reshape(peers * pitch, LANES)
    (back,) = kernel_call(
        functools.partial(back_kernel, width, groups, scale),
        [bf16(peers, 3 * width, LANES)],
        scratch=[scratch] * 4 + [pltpu.VMEM((LANES, LANES), F32)],
        count=5,
        mib=10,
    )(dconv, payload, saved, taps, table)
    back = exchange(back)
    part_width = width // groups
    part_scratch = pltpu.VMEM((peers * part_width, LANES), F32)
    part, grad_short = kernel_call(
        functools.partial(part_kernel, width, part_width),
        [bf16(peers * part_width, LANES), f32(3, FILT, channels)],
        scratch=[scratch, part_scratch],
        count=1,
    )(back)
    other = lax.ppermute(part, "dp", [(i, i ^ 1) for i in range(groups)])
    (grads,) = kernel_call(
        functools.partial(unpack_kernel, width), [bf16(3, 1, LANES, channels)], count=2
    )(back, grad_q)
    (grad_long,) = kernel_call(
        functools.partial(join_kernel, width, part_width),
        [f32(LANES, channels)],
        smem=(0,),
        scratch=[part_scratch, scratch],
        count=3,
    )(side, part, other)
    return (mixed[None], grads, grad_long, grad_short)


def solution(mesh):
    in_specs = (
        P("dp", "context", "tensor"),
        P("dp", "context", "tensor"),
        P("dp", "context", "tensor"),
        P(None, None, "tensor"),
        P("context", "tensor"),
        P("tensor"),
        P("dp", "context", "tensor"),
    )
    out_specs = (
        P("dp", "context", "tensor"),
        P(None, "dp", "context", "tensor"),
        P("context", "tensor"),
        P(None, None, "tensor"),
    )
    return jax.shard_map(shards, mesh=mesh, in_specs=in_specs, out_specs=out_specs, check_vma=False)
```

```python
import functools
import math

import jax
import jax.numpy as jnp
import numpy as np
from jax import lax
from jax.experimental import pallas as pl
from jax.experimental.pallas import tpu as pltpu
from jax.sharding import PartitionSpec as P

D = 4096
FILT = 7
EPS = 1e-06
LANES = 128
F32 = jnp.float32
BF16 = jnp.bfloat16
VMEM = pl.BlockSpec(memory_space=pltpu.VMEM)
SMEM = pl.BlockSpec(memory_space=pltpu.SMEM)


def halves(table):
    high = table.astype(jnp.bfloat16)
    low = (table - high.astype(np.float64)).astype(jnp.bfloat16)
    return high, low


@functools.cache
def tables(rows):
    size = rows * LANES
    row = np.arange(rows)
    lane = np.arange(LANES)
    angle = 2 * np.pi * np.outer(row + 0.25, row) / rows
    high, low = halves(np.concatenate([np.cos(angle), -np.sin(angle)], 0))
    first = np.concatenate([high, high, low], 1)
    high, low = halves(np.concatenate([np.cos(angle).T, np.sin(angle).T], 1) / size)
    last = np.concatenate([high, high, low], 1)
    turn = 2 * np.pi * np.outer(row + 0.25, lane) / size
    twiddle = np.concatenate([np.cos(turn), -np.sin(turn)], 1)
    twiddles = []
    for _ in range(3):
        twiddles.append(twiddle.astype(jnp.bfloat16))
        twiddle = twiddle - twiddles[-1].astype(np.float64)
    grid = 2 * np.pi * (np.outer(lane, lane) % LANES) / LANES
    cosine, sine = np.cos(grid), -np.sin(grid)
    inner = np.concatenate(halves(np.block([[cosine, sine], [-sine, cosine]])), 0)
    wide = lambda part: np.pad(part, ((0, 0), (0, 2 * LANES - part.shape[1])))
    return np.concatenate([inner, wide(first), wide(last[:, : 2 * LANES]), wide(last[:, 2 * LANES :])] + twiddles, 0)


class Tables:
    def __init__(self, ref, rows):
        self.ref, self.rows = ref, rows
        start = 4 * LANES + 4 * rows
        parts = [ref[start + index * rows : start + (index + 1) * rows, :].astype(F32) for index in range(3)]
        twiddle = parts[0] + parts[1] + parts[2]
        self.real, self.imag = twiddle[:, :LANES], twiddle[:, LANES:]

    def inner(self):
        high, low = self.ref[: 2 * LANES, :], self.ref[2 * LANES : 4 * LANES, :]
        return jnp.concatenate([high, high, low], 0)

    def first(self):
        return self.ref[4 * LANES : 4 * LANES + 2 * self.rows, : 3 * self.rows]

    def last(self):
        start, wide = 4 * LANES + 2 * self.rows, 6 * self.rows
        left = self.ref[start : start + self.rows, : min(wide, 2 * LANES)]
        if wide <= 2 * LANES:
            return left
        return jnp.concatenate([left, self.ref[start + self.rows : start + 2 * self.rows, : wide - 2 * LANES]], 1)

    def turned(self, real, imag):
        return real * self.real - imag * self.imag, real * self.imag + imag * self.real


def split(values):
    high = values.astype(BF16)
    return high, (values - high.astype(F32)).astype(BF16)


def dot(left, right):
    return jnp.dot(left, right, preferred_element_type=F32)


def along_lanes(values, table):
    high, low = split(values)
    return dot(jnp.concatenate([high, low, high], 1), table.inner())


def forward(blocks, table):
    rows = blocks[0].shape[0]
    parts = []
    for pair in range(0, len(blocks), 2):
        high, low = split(jnp.concatenate(blocks[pair : pair + 2], 1))
        mixed = dot(table.first(), jnp.concatenate([high, low, high], 0))
        for side in range(2):
            lanes = slice(side * LANES, (side + 1) * LANES)
            parts.append(jnp.concatenate(table.turned(mixed[:rows, lanes], mixed[rows:, lanes]), 1))
    return along_lanes(jnp.concatenate(parts, 0), table)


def inverse(conjugates, rows, table):
    values = along_lanes(conjugates, table)
    count = conjugates.shape[0] // rows
    blocks = []
    for pair in range(0, count, 2):
        sides = []
        for block in (pair, pair + 1):
            part = values[block * rows : (block + 1) * rows]
            sides.append(jnp.concatenate(table.turned(part[:, :LANES], part[:, LANES:]), 0))
        high, low = split(jnp.concatenate(sides, 1))
        out = dot(table.last(), jnp.concatenate([high, low, high], 0))
        blocks += [out[:, :LANES], out[:, LANES:]]
    return blocks


def times(left, right, conjugate):
    re_l, im_l = left[:, :LANES], left[:, LANES:]
    re_r, im_r = right[:, :LANES], right[:, LANES:]
    if conjugate:
        return jnp.concatenate([re_l * re_r + im_l * im_r, im_l * re_r - re_l * im_r], 1)
    return jnp.concatenate([re_l * re_r - im_l * im_r, -(re_l * im_r + im_l * re_r)], 1)


def lagged(values):
    above, block = values[:-1], values[1:]
    lane = lax.broadcasted_iota(jnp.int32, block.shape, 2)
    return [block] + [
        pltpu.roll(jnp.where(lane >= LANES - lag, above, block), lag, 2) for lag in range(1, FILT)
    ]


def led(values):
    block, below = values[:-1], values[1:]
    lane = lax.broadcasted_iota(jnp.int32, block.shape, 2)
    return [block] + [
        pltpu.roll(jnp.where(lane < lag, below, block), LANES - lag, 2) for lag in range(1, FILT)
    ]


def filtered(shifted, taps_ref, branch):
    total = shifted[0] * taps_ref[branch * FILT][None]
    for lag in range(1, FILT):
        total = total + shifted[lag] * taps_ref[branch * FILT + lag][None]
    return total


def strided(ref, start, count, step):
    return ref[pl.ds(start, count, stride=step), :]


def kernel_call(kernel, shapes, smem=(), scratch=(), count=0, mib=6):
    return pl.pallas_call(
        kernel,
        out_shape=shapes,
        in_specs=[SMEM if index in smem else VMEM for index in range(count)],
        out_specs=[VMEM] * len(shapes),
        scratch_shapes=list(scratch),
        compiler_params=pltpu.CompilerParams(vmem_limit_bytes=mib * 2**20),
    )


def f32(*dims):
    return jax.ShapeDtypeStruct(dims, F32)


def bf16(*dims):
    return jax.ShapeDtypeStruct(dims, BF16)


def pack_kernel(width, side_ref, k_ref, v_ref, filt_ref, out_ref):
    low_side = side_ref[0, 0] == 1
    for start in range(0, k_ref.shape[1], LANES):
        into = slice(start // width, (start + LANES) // width)
        for index, ref in enumerate((k_ref, v_ref, filt_ref)):
            block = ref[:, start : start + LANES].astype(F32).T
            if ref is filt_ref:
                block = block - jnp.where(low_side, block.astype(BF16).astype(F32), 0.0)
            out_ref[into, index * width : (index + 1) * width, :] = (
                block.astype(BF16).reshape(LANES // width, width, LANES)
            )


def shifted(values, lag):
    return values[lag : lag + LANES]


HALO = 8


def prepare_kernel(q_ref, halo_ref, grad_ref, taps_ref, gain_ref, q_short_ref, grad_z_ref):
    for start in range(0, q_ref.shape[1], LANES):
        lanes = slice(start, start + LANES)
        extended = jnp.concatenate([halo_ref[:, lanes], q_ref[:, lanes]], 0).astype(F32)
        total = jnp.zeros((LANES, LANES), F32)
        for lag in range(FILT):
            total = total + shifted(extended, HALO - lag) * taps_ref[lag : lag + 1, lanes]
        q_short_ref[lanes, :] = total.T
        grad_z_ref[lanes, :] = (grad_ref[:, lanes].astype(F32) * gain_ref[:, lanes]).T


STEP = 4
CHUNK = 8


def chunks(peers, groups):
    rows = peers // groups
    size = min(CHUNK, rows)
    for start in range(0, peers, size):
        yield start, size, start % rows == 0, (start + size) % rows == 0


def loaded(payload_ref, index, width, start, size, at_first):
    rows = slice(index * width, (index + 1) * width)
    if at_first:
        block = payload_ref[start : start + size, rows, :].astype(F32)
        return jnp.concatenate([jnp.zeros((1, width, LANES), F32), block], 0)
    return payload_ref[start - 1 : start + size, rows, :].astype(F32)


def make_inputs(payload_ref, taps_ref, width, groups, kv_ref, filt_ref):
    peers = payload_ref.shape[0]
    rows = peers // groups
    span = rows * width
    for start, size, at_first, _ in chunks(peers, groups):
        k_short = filtered(lagged(loaded(payload_ref, 0, width, start, size, at_first)), taps_ref, 1)
        v_short = filtered(lagged(loaded(payload_ref, 1, width, start, size, at_first)), taps_ref, 2)
        kv_ref[start * width : (start + size) * width, :] = (k_short * v_short).reshape(size * width, LANES)
    parts = payload_ref[:, 2 * width : 3 * width, :].astype(F32)
    filt_ref[...] = (parts[:rows] + parts[rows:]).reshape(span, LANES)
    return rows, span


def input_blocks(start, width, groups, rows, kv_ref, filt_ref):
    span = rows * width
    channels = range(start, start + STEP)
    blocks = [
        strided(kv_ref, group * span + channel, rows, width) for channel in channels for group in range(groups)
    ]
    return blocks + [strided(filt_ref, channel, rows, width) for channel in channels]


def conv_kernel(width, groups, payload_ref, taps_ref, table_ref,
                conv_ref, kv_ref, filt_ref):
    rows, span = make_inputs(payload_ref, taps_ref, width, groups, kv_ref, filt_ref)
    pairs = STEP * groups * rows
    table = Tables(table_ref, rows)
    for start in range(0, width, STEP):
        spec = forward(input_blocks(start, width, groups, rows, kv_ref, filt_ref), table)
        products = []
        for side in range(STEP):
            for group in range(groups):
                block = (side * groups + group) * rows
                filt = pairs + side * rows
                products.append(times(spec[block : block + rows], spec[filt : filt + rows], False))
        convs = inverse(jnp.concatenate(products, 0), rows, table)
        for side in range(STEP):
            for group in range(groups):
                conv_ref[pl.ds(group * span + start + side, rows, stride=width), :] = convs[side * groups + group]


def spectra_kernel(width, groups, payload_ref, taps_ref, table_ref, out_ref, kv_ref, filt_ref):
    rows, span = make_inputs(payload_ref, taps_ref, width, groups, kv_ref, filt_ref)
    pairs = STEP * groups * rows
    table = Tables(table_ref, rows)
    for start in range(0, width, STEP):
        spec = forward(input_blocks(start, width, groups, rows, kv_ref, filt_ref), table)
        out_ref[start * groups * rows : start * groups * rows + pairs, :] = spec[:pairs]
        below = groups * span + start * rows
        out_ref[below : below + STEP * rows, :] = spec[pairs:]


def stats_kernel(conv_ref, q_short_ref, grad_z_ref, stats_ref):
    squares = jnp.zeros((LANES, LANES), F32)
    prods = squares
    for start in range(0, conv_ref.shape[0], LANES):
        lanes = slice(start, start + LANES)
        y_out = q_short_ref[lanes, :] * conv_ref[lanes, :]
        squares = squares + y_out * y_out
        prods = prods + grad_z_ref[lanes, :] * y_out
    squares = jnp.sum(squares, 0, keepdims=True)
    prods = jnp.sum(prods, 0, keepdims=True)
    stats_ref[0:1, :] = squares
    stats_ref[1:2, :] = prods


def scales(stats_ref):
    rms = jnp.sqrt(stats_ref[0:1, :] / D + EPS)
    return rms, stats_ref[1:2, :] / (D * rms * rms * rms)


TAPS = 2 * HALO
EXTRA = 2
SUMS_TOP = 1e18
CONV_TOP = 6.4e7
DCONV_TOP = 4.6e8


def dconv_kernel(width, conv_ref, q_short_ref, grad_z_ref, stats_ref, q_ref, halo_ref, out_ref, edge_ref, rows_ref):
    rms, slope = scales(stats_ref)
    inverse_rms = 1.0 / rms
    pitch = width + EXTRA
    for start in range(0, conv_ref.shape[0], LANES):
        lanes = slice(start, start + LANES)
        q_short = q_short_ref[lanes, :]
        conv = conv_ref[lanes, :]
        grad_y = grad_z_ref[lanes, :] * inverse_rms - q_short * conv * slope
        dconv = grad_y * q_short
        for peer in range(LANES // width):
            into = (start // width + peer) * pitch
            out_ref[into : into + width, :] = dconv[peer * width : (peer + 1) * width]
        grad = (grad_y * conv).T
        edge_ref[:, lanes] = grad[:HALO]
        extended = jnp.concatenate([halo_ref[:, lanes], q_ref[:, lanes]], 0).astype(F32)
        sums = [
            jnp.sum(grad * shifted(extended, HALO - lag), 0, keepdims=True) for lag in range(FILT)
        ]
        rows_ref[lanes, :] = jnp.concatenate(sums + [jnp.zeros((LANES - FILT, LANES), F32)], 0).T
    peers = conv_ref.shape[0] // width
    total = strided(rows_ref, 0, peers, width)
    for channel in range(1, width):
        total = total + pltpu.roll(strided(rows_ref, channel, peers, width), channel * TAPS, 1)
    out_ref[pl.ds(width, peers, stride=pitch), :] = total * (DCONV_TOP / SUMS_TOP)
    out_ref[pl.ds(width + 1, peers, stride=pitch), :] = jnp.zeros_like(total)


def mixed_kernel(conv_ref, q_short_ref, stats_ref, gain_ref, mixed_ref):
    rms, _ = scales(stats_ref)
    for start in range(0, conv_ref.shape[0], LANES):
        lanes = slice(start, start + LANES)
        y_out = q_short_ref[lanes, :] * conv_ref[lanes, :]
        mixed_ref[:, lanes] = ((y_out / rms).T * gain_ref[:, lanes]).astype(BF16)


def grad_q_kernel(conv_ref, q_short_ref, grad_z_ref, stats_ref, edge_ref, taps_ref, out_ref):
    rms, slope = scales(stats_ref)
    inverse_rms = 1.0 / rms
    for start in range(0, conv_ref.shape[0], LANES):
        lanes = slice(start, start + LANES)
        conv = conv_ref[lanes, :]
        grad = (grad_z_ref[lanes, :] * inverse_rms - q_short_ref[lanes, :] * conv * slope) * conv
        extended = jnp.concatenate([grad.T, edge_ref[:, lanes]], 0)
        total = jnp.zeros((LANES, LANES), F32)
        for lag in range(FILT):
            total = total + shifted(extended, lag) * taps_ref[lag : lag + 1, lanes]
        out_ref[:, lanes] = total.astype(BF16)


def back_kernel(width, groups, scale, dconv_ref, payload_ref, saved_ref, taps_ref, table_ref, out_ref, dkv_ref, grad_k_ref, grad_v_ref, dfilt_ref, short_ref):
    peers = payload_ref.shape[0]
    rows = peers // groups
    span = rows * width
    part_width = width // groups
    pitch = width + EXTRA
    dfilt_ref[...] = jnp.zeros(dfilt_ref.shape, F32)
    table = Tables(table_ref, rows)
    for start in range(0, width, STEP):
        blocks = []
        for channel in range(start, start + STEP):
            for group in range(groups):
                blocks.append(strided(dconv_ref, group * rows * pitch + channel, rows, pitch))
        spec = forward(blocks, table)
        below = groups * span + start * rows
        spec_filt = saved_ref[below : below + STEP * rows, :]
        spec_kv = saved_ref[start * groups * rows : (start + STEP) * groups * rows, :]
        products = []
        filters = []
        for side in range(STEP):
            total = 0.0
            for group in range(groups):
                block = (side * groups + group) * rows
                part = spec[block : block + rows]
                products.append(times(spec_filt[side * rows : (side + 1) * rows], part, True))
                total = total + times(spec_kv[block : block + rows], part, True)
            filters.append(total)
        results = inverse(jnp.concatenate(products + filters, 0), rows, table)
        for side in range(STEP):
            channel = start + side
            target = channel // part_width * span + channel % part_width
            dfilt_ref[pl.ds(target, rows, stride=width), :] = results[STEP * groups + side] * scale
            for group in range(groups):
                place = group * span + channel
                dkv_ref[pl.ds(place, rows, stride=width), :] = results[side * groups + group]
    totals = [0.0] * (2 * FILT)
    for start, size, at_first, _ in chunks(peers, groups):
        into = slice(start * width, (start + size) * width)
        dkv = dkv_ref[into, :].reshape(size, width, LANES)
        k_lags = lagged(loaded(payload_ref, 0, width, start, size, at_first))
        v_lags = lagged(loaded(payload_ref, 1, width, start, size, at_first))
        grad_k = dkv * filtered(v_lags, taps_ref, 2)
        grad_v = dkv * filtered(k_lags, taps_ref, 1)
        grad_k_ref[into, :] = grad_k.reshape(size * width, LANES)
        grad_v_ref[into, :] = grad_v.reshape(size * width, LANES)
        for branch, (grad, lags) in enumerate(((grad_k, k_lags), (grad_v, v_lags))):
            for lag in range(FILT):
                totals[branch * FILT + lag] = totals[branch * FILT + lag] + jnp.sum(grad * lags[lag], axis=0)
    for start, size, _, at_last in chunks(peers, groups):
        for index, ref in enumerate((grad_k_ref, grad_v_ref)):
            if at_last:
                values = ref[start * width : (start + size) * width, :]
                values = jnp.concatenate([values, jnp.zeros((width, LANES), F32)], 0)
            else:
                values = ref[start * width : (start + size + 1) * width, :]
            grads = filtered(led(values.reshape(size + 1, width, LANES)), taps_ref, 1 + index)
            out_ref[start : start + size, index * width : (index + 1) * width, :] = grads.astype(BF16)
    short_ref[...] = jnp.zeros(short_ref.shape, F32)
    for tap, total in enumerate(totals):
        short_ref[pl.ds(tap, width, stride=TAPS), :] = total
    sums = strided(dconv_ref, width, peers, pitch) * (SUMS_TOP / DCONV_TOP)
    short = (jnp.sum(short_ref[...].T, axis=0, keepdims=True), jnp.sum(sums, axis=0, keepdims=True))
    for index, values in enumerate(short):
        values = values * scale
        high = values.astype(BF16).astype(F32)
        for row, part in enumerate((high, values - high)):
            start = part_width + 2 * index + row
            dfilt_ref[pl.ds(start, peers, stride=width), :] = jnp.broadcast_to(part, (peers, LANES))
    out_ref[:, 2 * width :, :] = dfilt_ref[...].reshape(peers, width, LANES).astype(BF16)


def part_kernel(width, part_width, payload_ref, part_ref, short_ref, rows_ref, out_ref):
    peers = payload_ref.shape[0]
    rows_ref[...] = payload_ref[:, 2 * width :, :].astype(F32).reshape(peers * width, LANES)
    for row in range(part_width):
        out_ref[pl.ds(row, peers, stride=part_width), :] = strided(rows_ref, row, peers, width)
    part_ref[...] = out_ref[...].astype(BF16)
    short_kv, short_q = (
        strided(rows_ref, start, peers, width) + strided(rows_ref, start + 1, peers, width)
        for start in (part_width, part_width + 2)
    )
    lane = lax.broadcasted_iota(jnp.int32, short_q.shape, 1)
    for channel in range(width):
        back = LANES - channel * TAPS
        rows_ref[pl.ds(channel, peers, stride=width), :] = jnp.where(
            lane < FILT, pltpu.roll(short_q, back % LANES, 1), pltpu.roll(short_kv, (back + FILT) % LANES, 1)
        )
    for start in range(0, short_ref.shape[2], LANES):
        block = rows_ref[start : start + LANES, :].T
        for branch in range(3):
            short_ref[branch, :, start : start + LANES] = block[branch * FILT : (branch + 1) * FILT]


def unpack_kernel(width, payload_ref, grad_q_ref, grads_ref):
    grads_ref[0, 0] = grad_q_ref[...]
    for start in range(0, grad_q_ref.shape[1], LANES):
        source = slice(start // width, (start + LANES) // width)
        for index in range(2):
            block = payload_ref[source, index * width : (index + 1) * width, :].astype(F32)
            grads_ref[1 + index, 0, :, start : start + LANES] = block.reshape(LANES, LANES).T.astype(BF16)


def join_kernel(width, part_width, side_ref, own_ref, other_ref, long_ref, from_ref, rows_ref):
    peers = long_ref.shape[1] // width
    for order, ref in ((side_ref[0, 0], own_ref), (1 - side_ref[0, 0], other_ref)):
        from_ref[...] = ref[...].astype(F32)
        for row in range(part_width):
            rows_ref[pl.ds(order * part_width + row, peers, stride=width), :] = strided(
                from_ref, row, peers, part_width
            )
    for start in range(0, long_ref.shape[1], LANES):
        long_ref[:, start : start + LANES] = rows_ref[start : start + LANES, :].T


def encode(values, top):
    root = lax.rsqrt(lax.rsqrt(jnp.abs(values))) * (60000.0 / top**0.25)
    return jnp.where(values < 0, -root, root).astype(jnp.float16)


def decode(code, top):
    root = code.astype(F32) * (top**0.25 / 60000.0)
    return root * jnp.abs(root) * (root * root)


PEERS = ("dp", "context")


def exchange(payload):
    return lax.all_to_all(payload, PEERS, split_axis=0, concat_axis=0, tiled=True)


def passed_along(values, by):
    size = lax.axis_size("context")
    pairs = [(i, i + by) for i in range(size) if 0 <= i + by < size]
    return lax.ppermute(values, "context", pairs)


def shards(q_in, k_in, v_in, short_filt, long_filt, norm_gain, grad_out):
    rows = lax.axis_size("context")
    groups = lax.axis_size("dp")
    peers = rows * groups
    channels = q_in.shape[2]
    width = channels // peers
    size = peers * width
    place = lax.axis_index(PEERS)
    table = jnp.asarray(tables(rows))
    scratch = pltpu.VMEM((size, LANES), F32)
    scale = 1.0 / math.sqrt(groups * rows * LANES)
    gain = norm_gain[None]
    taps_q = jnp.pad(short_filt[0], ((0, 1), (0, 0)))
    taps = lax.dynamic_index_in_dim(short_filt.reshape(3 * FILT, peers, width), place, 1, keepdims=False)
    taps = jnp.broadcast_to(taps[:, :, None], (3 * FILT, width, LANES))

    side = lax.axis_index("dp").astype(jnp.int32).reshape(1, 1)
    steps = min(4, channels // LANES)
    columns = pl.BlockSpec((LANES, channels // steps), lambda step: (0, step))
    payload = pl.pallas_call(
        functools.partial(pack_kernel, width),
        grid=(steps,),
        out_shape=bf16(peers, 3 * width, LANES),
        in_specs=[SMEM] + [columns] * 3,
        out_specs=pl.BlockSpec((peers // steps, 3 * width, LANES), lambda step: (step, 0, 0)),
        compiler_params=pltpu.CompilerParams(vmem_limit_bytes=56 * 2**20),
    )(side, k_in[0], v_in[0], long_filt)
    payload = exchange(payload)

    halo = passed_along(q_in[0, LANES - HALO :], 1)
    q_short, grad_z = kernel_call(prepare_kernel, [f32(channels, LANES)] * 2, count=5)(
        q_in[0], halo, grad_out[0], taps_q, gain
    )

    inputs = [scratch, pltpu.VMEM((rows * width, LANES), F32)]
    (conv,) = kernel_call(
        functools.partial(conv_kernel, width, groups),
        [f32(size, LANES)],
        scratch=inputs,
        count=3,
        mib=10,
    )(payload, taps, table)

    conv = exchange(encode(conv, CONV_TOP).reshape(peers, width, LANES))
    conv = decode(conv, CONV_TOP).reshape(size, LANES)
    (stats,) = kernel_call(stats_kernel, [f32(2, LANES)], count=3)(conv, q_short, grad_z)
    peer = 1
    while peer < lax.axis_size("tensor"):
        pairs = [(index, index ^ peer) for index in range(lax.axis_size("tensor"))]
        stats = stats + lax.ppermute(stats, "tensor", pairs)
        peer *= 2
    pitch = width + EXTRA
    dconv, edge = kernel_call(
        functools.partial(dconv_kernel, width),
        [f32(peers * pitch, LANES), f32(HALO, channels)],
        scratch=[scratch],
        count=6,
    )(conv, q_short, grad_z, stats, q_in[0], halo)
    code = exchange(encode(dconv, DCONV_TOP).reshape(peers, pitch // 2, 2, LANES)).reshape(peers * pitch, LANES)

    edge = passed_along(edge, -1)
    (mixed,) = kernel_call(mixed_kernel, [bf16(LANES, channels)], count=4)(conv, q_short, stats, gain)
    (grad_q,) = kernel_call(grad_q_kernel, [bf16(LANES, channels)], count=6)(
        conv, q_short, grad_z, stats, edge, taps_q
    )
    (saved,) = kernel_call(
        functools.partial(spectra_kernel, width, groups),
        [f32(size + rows * width, 2 * LANES)],
        scratch=inputs,
        count=3,
        mib=10,
    )(payload, taps, table)
    code, mixed, grad_q, saved = lax.optimization_barrier((code, mixed, grad_q, saved))

    dconv = decode(code, DCONV_TOP)
    (back,) = kernel_call(
        functools.partial(back_kernel, width, groups, scale),
        [bf16(peers, 3 * width, LANES)],
        scratch=[scratch] * 4 + [pltpu.VMEM((LANES, LANES), F32)],
        count=5,
        mib=10,
    )(dconv, payload, saved, taps, table)
    back = exchange(back)
    part_width = width // groups
    part_scratch = pltpu.VMEM((peers * part_width, LANES), F32)
    part, grad_short = kernel_call(
        functools.partial(part_kernel, width, part_width),
        [bf16(peers * part_width, LANES), f32(3, FILT, channels)],
        scratch=[scratch, part_scratch],
        count=1,
    )(back)
    other = lax.ppermute(part, "dp", [(i, i ^ 1) for i in range(groups)])
    (grads,) = kernel_call(
        functools.partial(unpack_kernel, width), [bf16(3, 1, LANES, channels)], count=2
    )(back, grad_q)
    (grad_long,) = kernel_call(
        functools.partial(join_kernel, width, part_width),
        [f32(LANES, channels)],
        smem=(0,),
        scratch=[part_scratch, scratch],
        count=3,
    )(side, part, other)
    return (mixed[None], grads, grad_long, grad_short)


def solution(mesh):
    in_specs = (
        P("dp", "context", "tensor"),
        P("dp", "context", "tensor"),
        P("dp", "context", "tensor"),
        P(None, None, "tensor"),
        P("context", "tensor"),
        P("tensor"),
        P("dp", "context", "tensor"),
    )
    out_specs = (
        P("dp", "context", "tensor"),
        P(None, "dp", "context", "tensor"),
        P("context", "tensor"),
        P(None, None, "tensor"),
    )
    return jax.shard_map(shards, mesh=mesh, in_specs=in_specs, out_specs=out_specs, check_vma=False)
```

```python
import functools
import math

import jax
import jax.numpy as jnp
import numpy as np
from jax import lax
from jax.experimental import pallas as pl
from jax.experimental.pallas import tpu as pltpu
from jax.sharding import PartitionSpec as P

D = 4096
FILT = 7
EPS = 1e-06
LANES = 128
F32 = jnp.float32
BF16 = jnp.bfloat16
VMEM = pl.BlockSpec(memory_space=pltpu.VMEM)
SMEM = pl.BlockSpec(memory_space=pltpu.SMEM)


def halves(table):
    high = table.astype(jnp.bfloat16)
    low = (table - high.astype(np.float64)).astype(jnp.bfloat16)
    return high, low


@functools.cache
def tables(rows):
    size = rows * LANES
    row = np.arange(rows)
    lane = np.arange(LANES)
    angle = 2 * np.pi * np.outer(row + 0.25, row) / rows
    high, low = halves(np.concatenate([np.cos(angle), -np.sin(angle)], 0))
    first = np.concatenate([high, high, low], 1)
    high, low = halves(np.concatenate([np.cos(angle).T, np.sin(angle).T], 1) / size)
    last = np.concatenate([high, high, low], 1)
    turn = 2 * np.pi * np.outer(row + 0.25, lane) / size
    twiddle = np.concatenate([np.cos(turn), -np.sin(turn)], 1)
    twiddles = []
    for _ in range(3):
        twiddles.append(twiddle.astype(jnp.bfloat16))
        twiddle = twiddle - twiddles[-1].astype(np.float64)
    grid = 2 * np.pi * (np.outer(lane, lane) % LANES) / LANES
    cosine, sine = np.cos(grid), -np.sin(grid)
    inner = np.concatenate(halves(np.block([[cosine, sine], [-sine, cosine]])), 0)
    wide = lambda part: np.pad(part, ((0, 0), (0, 2 * LANES - part.shape[1])))
    return np.concatenate([inner, wide(first), wide(last[:, : 2 * LANES]), wide(last[:, 2 * LANES :])] + twiddles, 0)


class Tables:
    def __init__(self, ref, rows):
        self.ref, self.rows = ref, rows
        start = 4 * LANES + 4 * rows
        parts = [ref[start + index * rows : start + (index + 1) * rows, :].astype(F32) for index in range(3)]
        twiddle = parts[0] + parts[1] + parts[2]
        self.real, self.imag = twiddle[:, :LANES], twiddle[:, LANES:]

    def inner(self):
        high, low = self.ref[: 2 * LANES, :], self.ref[2 * LANES : 4 * LANES, :]
        return jnp.concatenate([high, high, low], 0)

    def first(self):
        return self.ref[4 * LANES : 4 * LANES + 2 * self.rows, : 3 * self.rows]

    def last(self):
        start, wide = 4 * LANES + 2 * self.rows, 6 * self.rows
        left = self.ref[start : start + self.rows, : min(wide, 2 * LANES)]
        if wide <= 2 * LANES:
            return left
        return jnp.concatenate([left, self.ref[start + self.rows : start + 2 * self.rows, : wide - 2 * LANES]], 1)

    def turned(self, real, imag):
        return real * self.real - imag * self.imag, real * self.imag + imag * self.real


def split(values):
    high = values.astype(BF16)
    return high, (values - high.astype(F32)).astype(BF16)


def dot(left, right):
    return jnp.dot(left, right, preferred_element_type=F32)


def along_lanes(values, table):
    high, low = split(values)
    return dot(jnp.concatenate([high, low, high], 1), table.inner())


def forward(blocks, table):
    rows = blocks[0].shape[0]
    parts = []
    for pair in range(0, len(blocks), 2):
        high, low = split(jnp.concatenate(blocks[pair : pair + 2], 1))
        mixed = dot(table.first(), jnp.concatenate([high, low, high], 0))
        for side in range(2):
            lanes = slice(side * LANES, (side + 1) * LANES)
            parts.append(jnp.concatenate(table.turned(mixed[:rows, lanes], mixed[rows:, lanes]), 1))
    return along_lanes(jnp.concatenate(parts, 0), table)


def inverse(conjugates, rows, table):
    values = along_lanes(conjugates, table)
    count = conjugates.shape[0] // rows
    blocks = []
    for pair in range(0, count, 2):
        sides = []
        for block in (pair, pair + 1):
            part = values[block * rows : (block + 1) * rows]
            sides.append(jnp.concatenate(table.turned(part[:, :LANES], part[:, LANES:]), 0))
        high, low = split(jnp.concatenate(sides, 1))
        out = dot(table.last(), jnp.concatenate([high, low, high], 0))
        blocks += [out[:, :LANES], out[:, LANES:]]
    return blocks


def times(left, right, conjugate):
    re_l, im_l = left[:, :LANES], left[:, LANES:]
    re_r, im_r = right[:, :LANES], right[:, LANES:]
    if conjugate:
        return jnp.concatenate([re_l * re_r + im_l * im_r, im_l * re_r - re_l * im_r], 1)
    return jnp.concatenate([re_l * re_r - im_l * im_r, -(re_l * im_r + im_l * re_r)], 1)


def lagged(values):
    above, block = values[:-1], values[1:]
    lane = lax.broadcasted_iota(jnp.int32, block.shape, 2)
    return [block] + [
        pltpu.roll(jnp.where(lane >= LANES - lag, above, block), lag, 2) for lag in range(1, FILT)
    ]


def led(values):
    block, below = values[:-1], values[1:]
    lane = lax.broadcasted_iota(jnp.int32, block.shape, 2)
    return [block] + [
        pltpu.roll(jnp.where(lane < lag, below, block), LANES - lag, 2) for lag in range(1, FILT)
    ]


def filtered(shifted, taps_ref, branch):
    total = shifted[0] * taps_ref[branch * FILT][None]
    for lag in range(1, FILT):
        total = total + shifted[lag] * taps_ref[branch * FILT + lag][None]
    return total


def strided(ref, start, count, step):
    return ref[pl.ds(start, count, stride=step), :]


def kernel_call(kernel, shapes, smem=(), scratch=(), count=0, mib=6):
    return pl.pallas_call(
        kernel,
        out_shape=shapes,
        in_specs=[SMEM if index in smem else VMEM for index in range(count)],
        out_specs=[VMEM] * len(shapes),
        scratch_shapes=list(scratch),
        compiler_params=pltpu.CompilerParams(vmem_limit_bytes=mib * 2**20),
    )


def f32(*dims):
    return jax.ShapeDtypeStruct(dims, F32)


def bf16(*dims):
    return jax.ShapeDtypeStruct(dims, BF16)


def pack_kernel(width, side_ref, k_ref, v_ref, filt_ref, out_ref):
    low_side = side_ref[0, 0] == 1
    for start in range(0, k_ref.shape[1], LANES):
        into = slice(start // width, (start + LANES) // width)
        for index, ref in enumerate((k_ref, v_ref, filt_ref)):
            block = ref[:, start : start + LANES].astype(F32).T
            if ref is filt_ref:
                block = block - jnp.where(low_side, block.astype(BF16).astype(F32), 0.0)
            out_ref[into, index * width : (index + 1) * width, :] = (
                block.astype(BF16).reshape(LANES // width, width, LANES)
            )


def shifted(values, lag):
    return values[lag : lag + LANES]


HALO = 8


def prepare_kernel(q_ref, halo_ref, grad_ref, taps_ref, gain_ref, q_short_ref, grad_z_ref):
    for start in range(0, q_ref.shape[1], LANES):
        lanes = slice(start, start + LANES)
        extended = jnp.concatenate([halo_ref[:, lanes], q_ref[:, lanes]], 0).astype(F32)
        total = jnp.zeros((LANES, LANES), F32)
        for lag in range(FILT):
            total = total + shifted(extended, HALO - lag) * taps_ref[lag : lag + 1, lanes]
        q_short_ref[lanes, :] = total.T
        grad_z_ref[lanes, :] = (grad_ref[:, lanes].astype(F32) * gain_ref[:, lanes]).T


STEP = 4
CHUNK = 8


def chunks(peers, groups):
    rows = peers // groups
    size = min(CHUNK, rows)
    for start in range(0, peers, size):
        yield start, size, start % rows == 0, (start + size) % rows == 0


def loaded(payload_ref, index, width, start, size, at_first):
    rows = slice(index * width, (index + 1) * width)
    if at_first:
        block = payload_ref[start : start + size, rows, :].astype(F32)
        return jnp.concatenate([jnp.zeros((1, width, LANES), F32), block], 0)
    return payload_ref[start - 1 : start + size, rows, :].astype(F32)


def make_inputs(payload_ref, taps_ref, width, groups, kv_ref, filt_ref):
    peers = payload_ref.shape[0]
    rows = peers // groups
    span = rows * width
    for start, size, at_first, _ in chunks(peers, groups):
        k_short = filtered(lagged(loaded(payload_ref, 0, width, start, size, at_first)), taps_ref, 1)
        v_short = filtered(lagged(loaded(payload_ref, 1, width, start, size, at_first)), taps_ref, 2)
        kv_ref[start * width : (start + size) * width, :] = (k_short * v_short).reshape(size * width, LANES)
    parts = payload_ref[:, 2 * width : 3 * width, :].astype(F32)
    filt_ref[...] = (parts[:rows] + parts[rows:]).reshape(span, LANES)
    return rows, span


def input_blocks(start, width, groups, rows, kv_ref, filt_ref):
    span = rows * width
    channels = range(start, start + STEP)
    blocks = [
        strided(kv_ref, group * span + channel, rows, width) for channel in channels for group in range(groups)
    ]
    return blocks + [strided(filt_ref, channel, rows, width) for channel in channels]


def conv_kernel(width, groups, payload_ref, taps_ref, table_ref,
                conv_ref, kv_ref, filt_ref):
    rows, span = make_inputs(payload_ref, taps_ref, width, groups, kv_ref, filt_ref)
    pairs = STEP * groups * rows
    table = Tables(table_ref, rows)
    for start in range(0, width, STEP):
        spec = forward(input_blocks(start, width, groups, rows, kv_ref, filt_ref), table)
        products = []
        for side in range(STEP):
            for group in range(groups):
                block = (side * groups + group) * rows
                filt = pairs + side * rows
                products.append(times(spec[block : block + rows], spec[filt : filt + rows], False))
        convs = inverse(jnp.concatenate(products, 0), rows, table)
        for side in range(STEP):
            for group in range(groups):
                conv_ref[pl.ds(group * span + start + side, rows, stride=width), :] = convs[side * groups + group]


def spectra_kernel(width, groups, payload_ref, taps_ref, table_ref, out_ref, kv_ref, filt_ref):
    rows, span = make_inputs(payload_ref, taps_ref, width, groups, kv_ref, filt_ref)
    pairs = STEP * groups * rows
    table = Tables(table_ref, rows)
    for start in range(0, width, STEP):
        spec = forward(input_blocks(start, width, groups, rows, kv_ref, filt_ref), table)
        out_ref[start * groups * rows : start * groups * rows + pairs, :] = spec[:pairs]
        below = groups * span + start * rows
        out_ref[below : below + STEP * rows, :] = spec[pairs:]


def stats_kernel(conv_ref, q_short_ref, grad_z_ref, stats_ref):
    squares = jnp.zeros((LANES, LANES), F32)
    prods = squares
    for start in range(0, conv_ref.shape[0], LANES):
        lanes = slice(start, start + LANES)
        y_out = q_short_ref[lanes, :] * conv_ref[lanes, :]
        squares = squares + y_out * y_out
        prods = prods + grad_z_ref[lanes, :] * y_out
    squares = jnp.sum(squares, 0, keepdims=True)
    prods = jnp.sum(prods, 0, keepdims=True)
    for peer in range(stats_ref.shape[0]):
        stats_ref[peer, 0:1, :] = squares
        stats_ref[peer, 1:2, :] = prods


def scales(stats_ref):
    stats = jnp.sum(stats_ref[...], axis=0)
    rms = jnp.sqrt(stats[0:1] / D + EPS)
    return rms, stats[1:2] / (D * rms * rms * rms)


TAPS = 2 * HALO
EXTRA = 2
SUMS_TOP = 1e18
CONV_TOP = 6.4e7
DCONV_TOP = 4.6e8


def dconv_kernel(width, conv_ref, q_short_ref, grad_z_ref, stats_ref, q_ref, halo_ref, out_ref, edge_ref, rows_ref):
    rms, slope = scales(stats_ref)
    inverse_rms = 1.0 / rms
    pitch = width + EXTRA
    for start in range(0, conv_ref.shape[0], LANES):
        lanes = slice(start, start + LANES)
        q_short = q_short_ref[lanes, :]
        conv = conv_ref[lanes, :]
        grad_y = grad_z_ref[lanes, :] * inverse_rms - q_short * conv * slope
        dconv = grad_y * q_short
        for peer in range(LANES // width):
            into = (start // width + peer) * pitch
            out_ref[into : into + width, :] = dconv[peer * width : (peer + 1) * width]
        grad = (grad_y * conv).T
        edge_ref[:, lanes] = grad[:HALO]
        extended = jnp.concatenate([halo_ref[:, lanes], q_ref[:, lanes]], 0).astype(F32)
        sums = [
            jnp.sum(grad * shifted(extended, HALO - lag), 0, keepdims=True) for lag in range(FILT)
        ]
        rows_ref[lanes, :] = jnp.concatenate(sums + [jnp.zeros((LANES - FILT, LANES), F32)], 0).T
    peers = conv_ref.shape[0] // width
    total = strided(rows_ref, 0, peers, width)
    for channel in range(1, width):
        total = total + pltpu.roll(strided(rows_ref, channel, peers, width), channel * TAPS, 1)
    out_ref[pl.ds(width, peers, stride=pitch), :] = total * (DCONV_TOP / SUMS_TOP)
    out_ref[pl.ds(width + 1, peers, stride=pitch), :] = jnp.zeros_like(total)


def mixed_kernel(conv_ref, q_short_ref, stats_ref, gain_ref, mixed_ref):
    rms, _ = scales(stats_ref)
    for start in range(0, conv_ref.shape[0], LANES):
        lanes = slice(start, start + LANES)
        y_out = q_short_ref[lanes, :] * conv_ref[lanes, :]
        mixed_ref[:, lanes] = ((y_out / rms).T * gain_ref[:, lanes]).astype(BF16)


def grad_q_kernel(conv_ref, q_short_ref, grad_z_ref, stats_ref, edge_ref, taps_ref, out_ref):
    rms, slope = scales(stats_ref)
    inverse_rms = 1.0 / rms
    for start in range(0, conv_ref.shape[0], LANES):
        lanes = slice(start, start + LANES)
        conv = conv_ref[lanes, :]
        grad = (grad_z_ref[lanes, :] * inverse_rms - q_short_ref[lanes, :] * conv * slope) * conv
        extended = jnp.concatenate([grad.T, edge_ref[:, lanes]], 0)
        total = jnp.zeros((LANES, LANES), F32)
        for lag in range(FILT):
            total = total + shifted(extended, lag) * taps_ref[lag : lag + 1, lanes]
        out_ref[:, lanes] = total.astype(BF16)


def back_kernel(width, groups, scale, dconv_ref, payload_ref, saved_ref, taps_ref, table_ref, out_ref, dkv_ref, grad_k_ref, grad_v_ref, dfilt_ref, short_ref):
    peers = payload_ref.shape[0]
    rows = peers // groups
    span = rows * width
    part_width = width // groups
    pitch = width + EXTRA
    dfilt_ref[...] = jnp.zeros(dfilt_ref.shape, F32)
    table = Tables(table_ref, rows)
    for start in range(0, width, STEP):
        blocks = []
        for channel in range(start, start + STEP):
            for group in range(groups):
                blocks.append(strided(dconv_ref, group * rows * pitch + channel, rows, pitch))
        spec = forward(blocks, table)
        below = groups * span + start * rows
        spec_filt = saved_ref[below : below + STEP * rows, :]
        spec_kv = saved_ref[start * groups * rows : (start + STEP) * groups * rows, :]
        products = []
        filters = []
        for side in range(STEP):
            total = 0.0
            for group in range(groups):
                block = (side * groups + group) * rows
                part = spec[block : block + rows]
                products.append(times(spec_filt[side * rows : (side + 1) * rows], part, True))
                total = total + times(spec_kv[block : block + rows], part, True)
            filters.append(total)
        results = inverse(jnp.concatenate(products + filters, 0), rows, table)
        for side in range(STEP):
            channel = start + side
            target = channel // part_width * span + channel % part_width
            dfilt_ref[pl.ds(target, rows, stride=width), :] = results[STEP * groups + side] * scale
            for group in range(groups):
                place = group * span + channel
                dkv_ref[pl.ds(place, rows, stride=width), :] = results[side * groups + group]
    totals = [0.0] * (2 * FILT)
    for start, size, at_first, _ in chunks(peers, groups):
        into = slice(start * width, (start + size) * width)
        dkv = dkv_ref[into, :].reshape(size, width, LANES)
        k_lags = lagged(loaded(payload_ref, 0, width, start, size, at_first))
        v_lags = lagged(loaded(payload_ref, 1, width, start, size, at_first))
        grad_k = dkv * filtered(v_lags, taps_ref, 2)
        grad_v = dkv * filtered(k_lags, taps_ref, 1)
        grad_k_ref[into, :] = grad_k.reshape(size * width, LANES)
        grad_v_ref[into, :] = grad_v.reshape(size * width, LANES)
        for branch, (grad, lags) in enumerate(((grad_k, k_lags), (grad_v, v_lags))):
            for lag in range(FILT):
                totals[branch * FILT + lag] = totals[branch * FILT + lag] + jnp.sum(grad * lags[lag], axis=0)
    for start, size, _, at_last in chunks(peers, groups):
        for index, ref in enumerate((grad_k_ref, grad_v_ref)):
            if at_last:
                values = ref[start * width : (start + size) * width, :]
                values = jnp.concatenate([values, jnp.zeros((width, LANES), F32)], 0)
            else:
                values = ref[start * width : (start + size + 1) * width, :]
            grads = filtered(led(values.reshape(size + 1, width, LANES)), taps_ref, 1 + index)
            out_ref[start : start + size, index * width : (index + 1) * width, :] = grads.astype(BF16)
    short_ref[...] = jnp.zeros(short_ref.shape, F32)
    for tap, total in enumerate(totals):
        short_ref[pl.ds(tap, width, stride=TAPS), :] = total
    sums = strided(dconv_ref, width, peers, pitch) * (SUMS_TOP / DCONV_TOP)
    short = (jnp.sum(short_ref[...].T, axis=0, keepdims=True), jnp.sum(sums, axis=0, keepdims=True))
    for index, values in enumerate(short):
        values = values * scale
        high = values.astype(BF16).astype(F32)
        for row, part in enumerate((high, values - high)):
            start = part_width + 2 * index + row
            dfilt_ref[pl.ds(start, peers, stride=width), :] = jnp.broadcast_to(part, (peers, LANES))
    out_ref[:, 2 * width :, :] = dfilt_ref[...].reshape(peers, width, LANES).astype(BF16)


def part_kernel(width, part_width, payload_ref, part_ref, rows_ref, out_ref):
    peers = payload_ref.shape[0]
    rows_ref[...] = payload_ref[:, 2 * width :, :].astype(F32).reshape(peers * width, LANES)
    for row in range(part_width):
        out_ref[pl.ds(row, peers, stride=part_width), :] = strided(rows_ref, row, peers, width)
    part_ref[...] = out_ref[...].astype(BF16)


def unpack_kernel(width, part_width, payload_ref, grad_q_ref, grads_ref, short_ref, rows_ref):
    peers = payload_ref.shape[0]
    grads_ref[0, 0] = grad_q_ref[...]
    rows_ref[...] = payload_ref[:, 2 * width :, :].astype(F32).reshape(peers * width, LANES)
    short_kv, short_q = (
        strided(rows_ref, start, peers, width) + strided(rows_ref, start + 1, peers, width)
        for start in (part_width, part_width + 2)
    )
    lane = lax.broadcasted_iota(jnp.int32, short_q.shape, 1)
    for channel in range(width):
        back = LANES - channel * TAPS
        rows_ref[pl.ds(channel, peers, stride=width), :] = jnp.where(
            lane < FILT, pltpu.roll(short_q, back % LANES, 1), pltpu.roll(short_kv, (back + FILT) % LANES, 1)
        )
    for start in range(0, grad_q_ref.shape[1], LANES):
        lanes = slice(start, start + LANES)
        source = slice(start // width, (start + LANES) // width)
        for index in range(2):
            block = payload_ref[source, index * width : (index + 1) * width, :].astype(F32)
            grads_ref[1 + index, 0, :, lanes] = block.reshape(LANES, LANES).T.astype(BF16)
        block = rows_ref[lanes, :].T
        for branch in range(3):
            short_ref[branch, :, lanes] = block[branch * FILT : (branch + 1) * FILT]


def join_kernel(width, part_width, side_ref, own_ref, other_ref, long_ref, from_ref, rows_ref):
    peers = long_ref.shape[1] // width
    for order, ref in ((side_ref[0, 0], own_ref), (1 - side_ref[0, 0], other_ref)):
        from_ref[...] = ref[...].astype(F32)
        for row in range(part_width):
            rows_ref[pl.ds(order * part_width + row, peers, stride=width), :] = strided(
                from_ref, row, peers, part_width
            )
    for start in range(0, long_ref.shape[1], LANES):
        long_ref[:, start : start + LANES] = rows_ref[start : start + LANES, :].T


def encode(values, top):
    root = lax.rsqrt(lax.rsqrt(jnp.abs(values))) * (60000.0 / top**0.25)
    return jnp.where(values < 0, -root, root).astype(jnp.float16)


def decode(code, top):
    root = code.astype(F32) * (top**0.25 / 60000.0)
    return root * jnp.abs(root) * (root * root)


PEERS = ("dp", "context")


def exchange(payload):
    return lax.all_to_all(payload, PEERS, split_axis=0, concat_axis=0, tiled=True)


def passed_along(values, by):
    size = lax.axis_size("context")
    pairs = [(i, i + by) for i in range(size) if 0 <= i + by < size]
    return lax.ppermute(values, "context", pairs)


def shards(q_in, k_in, v_in, short_filt, long_filt, norm_gain, grad_out):
    rows = lax.axis_size("context")
    groups = lax.axis_size("dp")
    peers = rows * groups
    channels = q_in.shape[2]
    width = channels // peers
    size = peers * width
    place = lax.axis_index(PEERS)
    table = jnp.asarray(tables(rows))
    scratch = pltpu.VMEM((size, LANES), F32)
    scale = 1.0 / math.sqrt(groups * rows * LANES)
    gain = norm_gain[None]
    taps_q = jnp.pad(short_filt[0], ((0, 1), (0, 0)))
    taps = lax.dynamic_index_in_dim(short_filt.reshape(3 * FILT, peers, width), place, 1, keepdims=False)
    taps = jnp.broadcast_to(taps[:, :, None], (3 * FILT, width, LANES))

    side = lax.axis_index("dp").astype(jnp.int32).reshape(1, 1)
    (payload,) = kernel_call(
        functools.partial(pack_kernel, width), [bf16(peers, 3 * width, LANES)], smem=(0,), count=4, mib=56
    )(side, k_in[0], v_in[0], long_filt)
    payload = exchange(payload)

    halo = passed_along(q_in[0, LANES - HALO :], 1)
    q_short, grad_z = kernel_call(prepare_kernel, [f32(channels, LANES)] * 2, count=5)(
        q_in[0], halo, grad_out[0], taps_q, gain
    )

    inputs = [scratch, pltpu.VMEM((rows * width, LANES), F32)]
    (conv,) = kernel_call(
        functools.partial(conv_kernel, width, groups),
        [f32(size, LANES)],
        scratch=inputs,
        count=3,
        mib=10,
    )(payload, taps, table)

    conv = exchange(encode(conv, CONV_TOP).reshape(peers, width, LANES))
    conv = decode(conv, CONV_TOP).reshape(size, LANES)
    (stats,) = kernel_call(stats_kernel, [f32(lax.axis_size("tensor"), 2, LANES)], count=3)(conv, q_short, grad_z)
    stats = lax.all_to_all(stats, "tensor", split_axis=0, concat_axis=0, tiled=True)
    pitch = width + EXTRA
    dconv, edge = kernel_call(
        functools.partial(dconv_kernel, width),
        [f32(peers * pitch, LANES), f32(HALO, channels)],
        scratch=[scratch],
        count=6,
    )(conv, q_short, grad_z, stats, q_in[0], halo)
    code = exchange(encode(dconv, DCONV_TOP).reshape(peers, pitch // 2, 2, LANES)).reshape(peers * pitch, LANES)

    edge = passed_along(edge, -1)
    (mixed,) = kernel_call(mixed_kernel, [bf16(LANES, channels)], count=4)(conv, q_short, stats, gain)
    (grad_q,) = kernel_call(grad_q_kernel, [bf16(LANES, channels)], count=6)(
        conv, q_short, grad_z, stats, edge, taps_q
    )
    (saved,) = kernel_call(
        functools.partial(spectra_kernel, width, groups),
        [f32(size + rows * width, 2 * LANES)],
        scratch=inputs,
        count=3,
        mib=10,
    )(payload, taps, table)
    code, mixed, grad_q, saved = lax.optimization_barrier((code, mixed, grad_q, saved))

    dconv = decode(code, DCONV_TOP)
    (back,) = kernel_call(
        functools.partial(back_kernel, width, groups, scale),
        [bf16(peers, 3 * width, LANES)],
        scratch=[scratch] * 4 + [pltpu.VMEM((LANES, LANES), F32)],
        count=5,
        mib=10,
    )(dconv, payload, saved, taps, table)
    back = exchange(back)
    part_width = width // groups
    part_scratch = pltpu.VMEM((peers * part_width, LANES), F32)
    (part,) = kernel_call(
        functools.partial(part_kernel, width, part_width),
        [bf16(peers * part_width, LANES)],
        scratch=[scratch, part_scratch],
        count=1,
    )(back)
    other = lax.ppermute(part, "dp", [(i, i ^ 1) for i in range(groups)])
    grads, grad_short = kernel_call(
        functools.partial(unpack_kernel, width, part_width),
        [bf16(3, 1, LANES, channels), f32(3, FILT, channels)],
        scratch=[scratch],
        count=2,
    )(back, grad_q)
    (grad_long,) = kernel_call(
        functools.partial(join_kernel, width, part_width),
        [f32(LANES, channels)],
        smem=(0,),
        scratch=[part_scratch, scratch],
        count=3,
    )(side, part, other)
    return (mixed[None], grads, grad_long, grad_short)


def solution(mesh):
    in_specs = (
        P("dp", "context", "tensor"),
        P("dp", "context", "tensor"),
        P("dp", "context", "tensor"),
        P(None, None, "tensor"),
        P("context", "tensor"),
        P("tensor"),
        P("dp", "context", "tensor"),
    )
    out_specs = (
        P("dp", "context", "tensor"),
        P(None, "dp", "context", "tensor"),
        P("context", "tensor"),
        P(None, None, "tensor"),
    )
    return jax.shard_map(shards, mesh=mesh, in_specs=in_specs, out_specs=out_specs, check_vma=False)
```
